256 devices in a mesh: dp: 8 (over x, core), code: 32 (over z, y).
Axes of the slice: x: 4, y: 4, z: 8, core: 2. Of those that a mesh axis runs over, the one named last changes fastest.
Arguments:
- latents: bfloat16 [4096, 256], P(('dp', 'code')), may hold values from -1000 to 1000
- out_grad: bfloat16 [4096, 256], P(('dp', 'code')), may hold values from -6 to 6
- targets: int32 [4096], P('dp'), may hold values from 0 to 262143
- codebook: bfloat16 [262144, 256], P('code'), may hold values from -2 to 2
Outputs:
- latent_grad: bfloat16 [4096, 256], P(('dp', 'code'))
- codebook_grad: float32 [262144, 256], P(('code', 'dp'))
- token_loss: float32 [4096], P(('dp', 'code'))
The draws below stay inside these ranges and needn't reach their ends.
All inputs are finite; a program needn't handle non-finite values.
Results may differ from the reference program's by a relative error of at most 0.0042.
Values may be sent and summed in bfloat16 or wider, within the bound.
No kernel may reach another device: no remote copies, remote signals or barrier semaphores. Data moves between devices by JAX's collectives and lax.ppermute only.
A program may use at most 128 MiB of HBM per device.

```python
import jax
import jax.numpy as jnp
from jax import lax

D = 256
CODE_DEV = 8192
TOK_DEV = 512
TOKENS = 4096
CODES = 262144
N_DP = 8
N_CODE = 32


def shared_book(key):
    base_key = jax.random.fold_in(key, 11)
    entries = jax.random.normal(base_key, (CODES, D), jnp.float32) * D ** (-0.5)
    entries = jnp.clip(entries, -6.0 * D ** (-0.5), 6.0 * D ** (-0.5))
    return entries


def draw_codebook(key, part):
    return shared_book(key).astype(jnp.bfloat16)


def draw_latents(key, part):
    own_key = jax.random.fold_in(key, 12)
    values = jnp.clip(jax.random.normal(own_key, (TOKENS, D), jnp.float32) * 3.0, -18.0, 18.0)
    return values.astype(jnp.bfloat16)


def with_ends(drawn, key, least, high):
    longest = drawn.shape.index(max(drawn.shape))
    spots = []
    for shift in (0, 1):
        where = [jax.random.randint(jax.random.fold_in(key, axis), (), 0, length) for axis, length in enumerate(drawn.shape)]
        where[longest] = (where[longest] + shift) % drawn.shape[longest]
        spots.append(tuple(where))
    return drawn.at[spots[0]].set(least).at[spots[1]].set(high)


def block_levels(rng, shape, cuts, low, top_value):
    def one(position, blocks):
        steps = jax.random.uniform(jax.random.fold_in(jax.random.fold_in(rng, 6), position), (blocks,), jnp.float32, low / len(cuts), top_value / len(cuts))
        return jnp.repeat(jnp.exp(steps), shape[position] // blocks).reshape((-1,) + (1,) * (len(shape) - position - 1))

    factor_of = one(*cuts[0])
    for cut in cuts[1:]:
        factor_of = factor_of * one(*cut)
    return factor_of


def gaussian(key, dims, width, most, cuts=(), kind=jnp.bfloat16):
    loudness = block_levels(key, dims, cuts, -0.22, 0.18) if cuts else 1.0
    values = jax.random.normal(key, dims, jnp.float32) * width * loudness
    return jnp.minimum(jnp.maximum(values, -most), most).astype(kind)


def setup_inputs(seed: int = 0) -> dict:
    arg_keys = jax.random.split(jax.random.key(seed), 5)
    return {
        "latents": draw_latents(jax.random.fold_in(arg_keys[4], 71), 0),
        "out_grad": gaussian(arg_keys[1], (TOKENS, D), 1.0, 6.0, ((0, 256),)),
        "targets": with_ends(jax.random.randint(arg_keys[2], (TOKENS,), 0, CODES), jax.random.fold_in(arg_keys[2], 1), 0, CODES - 1).astype(jnp.int32),
        "codebook": draw_codebook(jax.random.fold_in(arg_keys[4], 71), 0),
    }


ce_weight = 1.0


def reference(latents, out_grad, targets, codebook):
    hi = lax.Precision.HIGHEST
    lat_f = latents.astype(jnp.float32)
    grad_f = out_grad.astype(jnp.float32)
    book_f = codebook.astype(jnp.float32).reshape(N_CODE, CODE_DEV, D)
    offsets = jnp.arange(N_CODE, dtype=jnp.int32) * CODE_DEV

    def scores(book_block):
        return (jnp.dot(lat_f, book_block.T, precision=hi), jnp.dot(grad_f, book_block.T, precision=hi))

    def first_pass(carry, item):
        top, total, weighted, picked = carry
        book_block, offset = item
        logit_block, back_block = scores(book_block)
        new_top = jnp.maximum(top, jnp.max(logit_block, axis=1))
        factor = jnp.exp(top - new_top)
        expo = jnp.exp(logit_block - new_top[:, None])
        code_ids = offset + jnp.arange(CODE_DEV, dtype=jnp.int32)
        hit_mask = targets[:, None] == code_ids[None, :]
        total = total * factor + jnp.sum(expo, axis=1)
        weighted = weighted * factor + jnp.sum(expo * back_block, axis=1)
        picked = picked + jnp.sum(jnp.where(hit_mask, logit_block, 0.0), axis=1)
        return (new_top, total, weighted, picked), None

    zeros_tok = jnp.zeros((TOKENS,), jnp.float32)
    start = (jnp.full((TOKENS,), -jnp.inf, jnp.float32), zeros_tok, zeros_tok, zeros_tok)
    (top, total, weighted, picked), _ = lax.scan(first_pass, start, (book_f, offsets))
    lse = top + jnp.log(total)
    mean_back = weighted / total
    token_loss = lse - picked

    def second_pass(carry, item):
        book_block, offset = item
        logit_block, back_block = scores(book_block)
        probs = jnp.exp(logit_block - lse[:, None])
        code_ids = offset + jnp.arange(CODE_DEV, dtype=jnp.int32)
        onehot = (targets[:, None] == code_ids[None, :]).astype(jnp.float32)
        delta = probs * (back_block - mean_back[:, None]) + ce_weight * (probs - onehot)
        delta = delta.astype(jnp.bfloat16).astype(jnp.float32)
        carry = carry + jnp.dot(delta, book_block, precision=hi)
        delta_groups = delta.reshape(N_DP, TOK_DEV, CODE_DEV)
        onehot_groups = onehot.reshape(N_DP, TOK_DEV, CODE_DEV)
        parts = jnp.einsum("gtk,gtd->gkd", delta_groups, lat_f.reshape(N_DP, TOK_DEV, D), precision=hi)
        parts = parts + jnp.einsum("gtk,gtd->gkd", onehot_groups, grad_f.reshape(N_DP, TOK_DEV, D), precision=hi)
        return carry, jnp.sum(parts, axis=0)

    lat_grad, book_grad = lax.scan(second_pass, jnp.zeros((TOKENS, D), jnp.float32), (book_f, offsets))
    return lat_grad.astype(jnp.bfloat16), book_grad.reshape(CODES, D), token_loss
```

```python
import functools

import jax
import jax.numpy as jnp
from jax import lax
from jax.experimental import pallas as pl
from jax.experimental.pallas import tpu as pltpu
from jax.sharding import Mesh
from jax.sharding import PartitionSpec as P

ce_weight = 1.0
F32 = jnp.float32
BF16 = jnp.bfloat16
NT = (((1,), (1,)), ((), ()))
NN = (((1,), (0,)), ((), ()))
ZY = ("z", "y")


def dot(a, b, dims, precision=None):
    return lax.dot_general(a, b, dims, preferred_element_type=F32, precision=precision)


def params(**kw):
    return pltpu.CompilerParams(dimension_semantics=("arbitrary",), **kw)


def cost(flops, bytes_accessed, trans=0):
    return pl.CostEstimate(flops=flops, bytes_accessed=bytes_accessed, transcendentals=trans)


def pick_kernel(cb, tgt_ref, book_ref, out_ref):
    i = pl.program_id(0)

    @pl.when(i == 0)
    def _():
        out_ref[...] = jnp.zeros_like(out_ref)

    tokens = tgt_ref.shape[0]
    ids = lax.broadcasted_iota(jnp.int32, (tokens, cb), 1) + i * cb
    hit = jnp.where(ids == tgt_ref[:, :1], 1.0, 0.0).astype(BF16)
    out_ref[...] += dot(hit, book_ref[...], NN)


def pick_rows(tgt_cols, book):
    tokens, codes, d = tgt_cols.shape[0], *book.shape
    cb = 1024
    return pl.pallas_call(
        functools.partial(pick_kernel, cb),
        grid=(codes // cb,),
        in_specs=[
            pl.BlockSpec((tokens, 128), lambda i: (0, 0)),
            pl.BlockSpec((cb, d), lambda i: (i, 0)),
        ],
        out_specs=pl.BlockSpec((tokens, d), lambda i: (0, 0)),
        out_shape=jax.ShapeDtypeStruct((tokens, d), F32),
        compiler_params=params(),
        cost_estimate=cost(2 * tokens * codes * d, codes * d * 2),
        name="pick",
    )(tgt_cols, book)


def stats_kernel(steps, lat_ref, grad_ref, rows_ref, book_ref, out_ref, m_col, mean_col, m_s, l_s, w_s):
    i = pl.program_id(0)

    @pl.when(i == 0)
    def _():
        m_s[...] = jnp.full_like(m_s, -jnp.inf)
        l_s[...] = jnp.zeros_like(l_s)
        w_s[...] = jnp.zeros_like(w_s)

    block = book_ref[...]
    cb, tokens = block.shape[0], lat_ref.shape[0]
    logit = dot(block, lat_ref[...], NT).reshape(cb // 8, 8, tokens)
    back = dot(block, grad_ref[...], NT).reshape(cb // 8, 8, tokens)
    old = m_s[...]
    new = jnp.maximum(old, jnp.max(logit, axis=0))
    factor = jnp.exp(old - new)
    expo = jnp.exp(logit - new[None])
    l_s[...] = l_s[...] * factor + jnp.sum(expo, axis=0)
    w_s[...] = w_s[...] * factor + jnp.sum(expo * back, axis=0)
    m_s[...] = new

    @pl.when(i == steps - 1)
    def _():
        m = m_s[...]
        top = jnp.max(m, axis=0, keepdims=True)
        scale = jnp.exp(m - top)
        total = jnp.sum(l_s[...] * scale, axis=0, keepdims=True)
        weighted = jnp.sum(w_s[...] * scale, axis=0, keepdims=True)
        prod = lat_ref[...].astype(F32) * rows_ref[...]
        picked = dot(jnp.ones((8, prod.shape[1]), F32), prod, NT, lax.Precision.HIGHEST)[:1]
        pack = jnp.concatenate([top, total, weighted, picked], axis=0)
        out_ref[...] = jnp.broadcast_to(pack[None], out_ref.shape)
        m_col[...] = jnp.broadcast_to(top, (128, tokens)).T
        mean_col[...] = jnp.broadcast_to(weighted / total, (128, tokens)).T


def local_stats(toks, rows, book, peers):
    tokens, (codes, d) = toks.shape[0], book.shape
    cb = 1024
    steps = codes // cb
    return pl.pallas_call(
        functools.partial(stats_kernel, steps),
        grid=(steps,),
        in_specs=[
            pl.BlockSpec((tokens, d), lambda i: (0, 0)),
            pl.BlockSpec((tokens, d), lambda i: (0, 1)),
            pl.BlockSpec((tokens, d), lambda i: (0, 0)),
            pl.BlockSpec((cb, d), lambda i: (i, 0)),
        ],
        out_specs=[
            pl.BlockSpec((peers, 4, tokens), lambda i: (0, 0, 0)),
            pl.BlockSpec((tokens, 128), lambda i: (0, 0)),
            pl.BlockSpec((tokens, 128), lambda i: (0, 0)),
        ],
        out_shape=[
            jax.ShapeDtypeStruct((peers, 4, tokens), F32),
            jax.ShapeDtypeStruct((tokens, 128), F32),
            jax.ShapeDtypeStruct((tokens, 128), F32),
        ],
        scratch_shapes=[pltpu.VMEM((8, tokens), F32)] * 3,
        compiler_params=params(),
        cost_estimate=cost(4 * tokens * codes * d, codes * d * 2, tokens * codes),
        name="stats",
    )(toks, toks, rows, book)


def lat_kernel(lat_ref, grad_ref, m_ref, mean_ref, book_ref, a_ref, b_ref):
    i = pl.program_id(0)

    @pl.when(i == 0)
    def _():
        a_ref[...] = jnp.zeros_like(a_ref)
        b_ref[...] = jnp.zeros_like(b_ref)

    block = book_ref[...]
    logit = dot(lat_ref[...], block, NT)
    back = dot(grad_ref[...], block, NT)
    expo = jnp.exp(logit - m_ref[:, :1])
    dev = expo * (back - mean_ref[:, :1])
    a_ref[...] += dot(dev.astype(BF16), block, NN)
    b_ref[...] += dot(expo.astype(BF16), block, NN)


def local_lat(toks, m_col, mean_col, book):
    tokens, (codes, d) = toks.shape[0], book.shape
    cb = 1024
    return pl.pallas_call(
        lat_kernel,
        grid=(codes // cb,),
        in_specs=[
            pl.BlockSpec((tokens, d), lambda i: (0, 0)),
            pl.BlockSpec((tokens, d), lambda i: (0, 1)),
            pl.BlockSpec((tokens, 128), lambda i: (0, 0)),
            pl.BlockSpec((tokens, 128), lambda i: (0, 0)),
            pl.BlockSpec((cb, d), lambda i: (i, 0)),
        ],
        out_specs=[pl.BlockSpec((tokens, d), lambda i: (0, 0))] * 2,
        out_shape=[jax.ShapeDtypeStruct((tokens, d), F32)] * 2,
        compiler_params=params(),
        cost_estimate=cost(8 * tokens * codes * d, codes * d * 2, tokens * codes),
        name="local_lat",
    )(toks, toks, m_col, mean_col, book)


def combine_kernel(all_ref, m_col, mean_col, a_ref, b_ref, rows_ref, part_ref, row_ref, loss_ref):
    stats = all_ref[...]
    m, l, w = stats[:, 0, :], stats[:, 1, :], stats[:, 2, :]
    tokens = m.shape[1]
    top = jnp.max(m, axis=0, keepdims=True)
    scale = jnp.exp(m - top)
    total = jnp.sum(l * scale, axis=0, keepdims=True)
    mean = jnp.sum(w * scale, axis=0, keepdims=True) / total
    lse = top + jnp.log(total)
    row_ref[...] = jnp.concatenate([lse, mean], axis=0)
    loss_ref[...] = lse - jnp.sum(stats[:, 3, :], axis=0, keepdims=True)
    lse_col = jnp.broadcast_to(lse, (128, tokens)).T
    mean_all = jnp.broadcast_to(mean, (128, tokens)).T
    own = jnp.exp(m_col[...] - lse_col)
    ratio = own * (ce_weight + mean_col[...] - mean_all)
    part = own[:, :1] * a_ref[...] + ratio[:, :1] * b_ref[...] - ce_weight * rows_ref[...]
    part_ref[...] = part.astype(part_ref.dtype)


def combine(stats, m_col, mean_col, a, b, rows):
    tokens, d = a.shape
    return pl.pallas_call(
        combine_kernel,
        out_shape=[
            jax.ShapeDtypeStruct((tokens, d), F32),
            jax.ShapeDtypeStruct((2, tokens), F32),
            jax.ShapeDtypeStruct((1, tokens), F32),
        ],
        cost_estimate=cost(tokens * d * 8, tokens * d * 16),
        name="combine",
    )(stats, m_col, mean_col, a, b, rows)


def book_kernel(has_recv, cb, s_ref, lat_ref, grad_ref, row_ref, tgt_ref, book_ref, *rest):
    out_ref = rest[-1]
    i = pl.program_id(0)
    block = book_ref[...]
    tokens = lat_ref.shape[0]
    logit = dot(block, lat_ref[...], NT)
    back = dot(block, grad_ref[...], NT)
    prob = jnp.exp(logit - row_ref[0:1, :])
    ids = lax.broadcasted_iota(jnp.int32, (cb, tokens), 0) + (s_ref[0] * 1024 + i * cb)
    hit = jnp.where(ids == tgt_ref[...], 1.0, 0.0)
    delta = prob * (back - row_ref[1:2, :]) + ce_weight * (prob - hit)
    out = dot(delta.astype(BF16), lat_ref[...], NN) + dot(hit.astype(BF16), grad_ref[...], NN)
    if has_recv:
        out = out + rest[0][...].astype(F32)
    out_ref[...] = out.astype(out_ref.dtype)


def book_part(index, toks, row, tgt_row, book, recv, dtype):
    tokens, (codes, d) = toks.shape[0], book.shape
    chunk, cb = 1024, 512
    per = chunk // cb
    extra = [] if recv is None else [recv]
    grid_spec = pltpu.PrefetchScalarGridSpec(
        num_scalar_prefetch=1,
        grid=(per,),
        in_specs=[
            pl.BlockSpec((tokens, d), lambda i, s: (0, 0)),
            pl.BlockSpec((tokens, d), lambda i, s: (0, 1)),
            pl.BlockSpec((2, tokens), lambda i, s: (0, 0)),
            pl.BlockSpec((1, tokens), lambda i, s: (0, 0)),
            pl.BlockSpec((cb, d), lambda i, s: (s[0] * per + i, 0)),
        ]
        + [pl.BlockSpec((cb, d), lambda i, s: (i, 0)) for _ in extra],
        out_specs=pl.BlockSpec((cb, d), lambda i, s: (i, 0)),
    )
    return pl.pallas_call(
        functools.partial(book_kernel, recv is not None, cb),
        grid_spec=grid_spec,
        out_shape=jax.ShapeDtypeStruct((chunk, d), dtype),
        compiler_params=params(),
        cost_estimate=cost(8 * tokens * chunk * d, chunk * d * 6 + tokens * d * 4, tokens * chunk),
        name="book_part",
    )(index, toks, toks, row, tgt_row, book, *extra)


def per_device(latents, out_grad, targets, codebook):
    peers = lax.axis_size("z") * lax.axis_size("y")
    nx = lax.axis_size("x")
    own_count, d = latents.shape
    code_dev = codebook.shape[0]
    tokens = own_count * peers
    code_pos = lax.axis_index(ZY)
    x_pos, core = lax.axis_index("x"), lax.axis_index("core")

    both = jnp.concatenate([latents, out_grad], axis=1)
    toks = lax.all_to_all(jnp.broadcast_to(both[None], (peers, own_count, 2 * d)), ZY, 0, 0)
    toks = toks.reshape(tokens, 2 * d)
    local_ids = targets - code_pos * code_dev
    rows = pick_rows(jnp.broadcast_to(local_ids[:, None], (tokens, 128)), codebook)
    packed, m_col, mean_col = local_stats(toks, rows, codebook, peers)
    stats = lax.all_to_all(packed, ZY, 0, 0)
    a, b = local_lat(toks, m_col, mean_col, codebook)
    part, row, loss = combine(stats, m_col, mean_col, a, b, rows)
    moved = lax.all_to_all(part.reshape(peers, own_count, d), ZY, 0, 0)
    latent_grad = jnp.sum(moved, axis=0).astype(BF16)
    token_loss = lax.dynamic_slice(loss, (0, code_pos * own_count), (1, own_count)).reshape(own_count)

    tgt_row = local_ids[None, :]
    swap = [(0, 1), (1, 0)]

    def ring(k):
        return [(i, (i + k) % nx) for i in range(nx)]

    def index(k, same):
        chip = lax.rem(x_pos + k, nx)
        return (chip * 2 + (core if same else 1 - core)).astype(jnp.int32).reshape(1)

    def send(k):
        piece = book_part(index(k, False), toks, row, tgt_row, codebook, None, BF16)
        return lax.ppermute(piece, "core", swap)

    def keep(k, recv, dtype):
        return book_part(index(k, True), toks, row, tgt_row, codebook, recv, dtype)

    got = []
    for k in (2, 1, 3):
        got.append(lax.ppermute(keep(k, send(k), BF16), "x", ring(k)))
    own = keep(0, send(0), F32)
    codebook_grad = own + got[0].astype(F32) + got[1].astype(F32) + got[2].astype(F32)
    return latent_grad, codebook_grad, token_loss


def solution(mesh):
    shape = (mesh.shape["dp"] // 2, 2, mesh.shape["code"] // 4, 4)
    fine = Mesh(mesh.devices.reshape(shape), ("x", "core", "z", "y"))
    dp, code = ("x", "core"), ("z", "y")
    in_specs = (P(dp + code, None), P(dp + code, None), P(dp), P(code, None))
    out_specs = (P(dp + code, None), P(code + dp, None), P(dp + code))
    return jax.shard_map(
        per_device, mesh=fine, in_specs=in_specs, out_specs=out_specs, check_vma=False
    )
```

```python
import functools

import jax
import jax.numpy as jnp
from jax import lax
from jax.experimental import pallas as pl
from jax.experimental.pallas import tpu as pltpu
from jax.sharding import Mesh
from jax.sharding import PartitionSpec as P

ce_weight = 1.0
F32 = jnp.float32
BF16 = jnp.bfloat16
NT = (((1,), (1,)), ((), ()))
NN = (((1,), (0,)), ((), ()))
ZY = ("z", "y")
XC = ("x", "core")
VMEM_LIMIT = 32 << 20


def dot(a, b, dims, precision=None):
    return lax.dot_general(a, b, dims, preferred_element_type=F32, precision=precision)


def params(**kw):
    return pltpu.CompilerParams(vmem_limit_bytes=VMEM_LIMIT, **kw)


def cost(flops, bytes_accessed, trans=0):
    return pl.CostEstimate(flops=flops, bytes_accessed=bytes_accessed, transcendentals=trans)


def pick_kernel(cb, tgt_ref, book_ref, out_ref):
    i = pl.program_id(0)

    @pl.when(i == 0)
    def _():
        out_ref[...] = jnp.zeros_like(out_ref)

    tokens = tgt_ref.shape[0]
    ids = lax.broadcasted_iota(jnp.int32, (tokens, cb), 1) + i * cb
    hit = jnp.where(ids == tgt_ref[:, :1], 1.0, 0.0).astype(BF16)
    out_ref[...] += dot(hit, book_ref[...], NN)


def pick_rows(tgt_cols, book):
    tokens, codes, d = tgt_cols.shape[0], *book.shape
    cb = 1024
    return pl.pallas_call(
        functools.partial(pick_kernel, cb),
        grid=(codes // cb,),
        in_specs=[
            pl.BlockSpec((tokens, 128), lambda i: (0, 0)),
            pl.BlockSpec((cb, d), lambda i: (i, 0)),
        ],
        out_specs=pl.BlockSpec((tokens, d), lambda i: (0, 0)),
        out_shape=pltpu.HBM((tokens, d), F32),
        compiler_params=params(),
        cost_estimate=cost(2 * tokens * codes * d, codes * d * 2),
        name="pick",
    )(tgt_cols, book)


def stats_kernel(steps, lat_ref, grad_ref, rows_ref, book_ref, out_ref, m_col, mean_col, m_s, l_s, w_s):
    i = pl.program_id(0)

    @pl.when(i == 0)
    def _():
        m_s[...] = jnp.full_like(m_s, -jnp.inf)
        l_s[...] = jnp.zeros_like(l_s)
        w_s[...] = jnp.zeros_like(w_s)

    block = book_ref[...]
    cb, tokens = block.shape[0], lat_ref.shape[0]
    logit = dot(block, lat_ref[...], NT).reshape(cb // 8, 8, tokens)
    back = dot(block, grad_ref[...], NT).reshape(cb // 8, 8, tokens)
    old = m_s[...]
    new = jnp.maximum(old, jnp.max(logit, axis=0))
    factor = jnp.exp(old - new)
    expo = jnp.exp(logit - new[None])
    l_s[...] = l_s[...] * factor + jnp.sum(expo, axis=0)
    w_s[...] = w_s[...] * factor + jnp.sum(expo * back, axis=0)
    m_s[...] = new

    @pl.when(i == steps - 1)
    def _():
        m = m_s[...]
        top = jnp.max(m, axis=0, keepdims=True)
        scale = jnp.exp(m - top)
        total = jnp.sum(l_s[...] * scale, axis=0, keepdims=True)
        weighted = jnp.sum(w_s[...] * scale, axis=0, keepdims=True)
        prod = lat_ref[...].astype(F32) * rows_ref[...]
        picked = dot(jnp.ones((8, prod.shape[1]), F32), prod, NT, lax.Precision.HIGHEST)[:1]
        pack = jnp.concatenate([top, total, weighted, picked], axis=0)
        out_ref[...] = jnp.broadcast_to(pack[None], out_ref.shape)
        m_col[...] = jnp.broadcast_to(top, (128, tokens)).T
        mean_col[...] = jnp.broadcast_to(weighted / total, (128, tokens)).T


def local_stats(toks, rows, book, peers):
    tokens, (codes, d) = toks.shape[0], book.shape
    cb = 1024
    steps = codes // cb
    return pl.pallas_call(
        functools.partial(stats_kernel, steps),
        grid=(steps,),
        in_specs=[
            pl.BlockSpec((tokens, d), lambda i: (0, 0)),
            pl.BlockSpec((tokens, d), lambda i: (0, 1)),
            pl.BlockSpec((tokens, d), lambda i: (0, 0)),
            pl.BlockSpec((cb, d), lambda i: (i, 0)),
        ],
        out_specs=[
            pl.BlockSpec((peers, 4, tokens), lambda i: (0, 0, 0)),
            pl.BlockSpec((tokens, 128), lambda i: (0, 0)),
            pl.BlockSpec((tokens, 128), lambda i: (0, 0)),
        ],
        out_shape=[
            jax.ShapeDtypeStruct((peers, 4, tokens), F32),
            pltpu.HBM((tokens, 128), F32),
            pltpu.HBM((tokens, 128), F32),
        ],
        scratch_shapes=[pltpu.VMEM((8, tokens), F32)] * 3,
        compiler_params=params(),
        cost_estimate=cost(4 * tokens * codes * d, codes * d * 2, tokens * codes),
        name="stats",
    )(toks, toks, rows, book)


def lat_step(lat_ref, grad_ref, m_ref, mean_ref, book_ref, a_ref, b_ref):
    block = book_ref[...]
    logit = dot(lat_ref[...], block, NT)
    back = dot(grad_ref[...], block, NT)
    expo = jnp.exp(logit - m_ref[:, :1])
    dev = expo * (back - mean_ref[:, :1])
    a_ref[...] += dot(dev.astype(BF16), block, NN)
    b_ref[...] += dot(expo.astype(BF16), block, NN)


def first_kernel(lat_ref, grad_ref, m_ref, mean_ref, book_ref, a_ref, b_ref):
    @pl.when(pl.program_id(0) == 0)
    def _():
        a_ref[...] = jnp.zeros_like(a_ref)
        b_ref[...] = jnp.zeros_like(b_ref)

    lat_step(lat_ref, grad_ref, m_ref, mean_ref, book_ref, a_ref, b_ref)


def second_kernel(
    steps, lat_ref, grad_ref, m_ref, mean_ref, book_ref, a0, b0, rows_ref, all_ref, part_ref, a_ref, b_ref
):
    @pl.when(pl.program_id(0) == 0)
    def _():
        a_ref[...] = a0[...]
        b_ref[...] = b0[...]

    lat_step(lat_ref, grad_ref, m_ref, mean_ref, book_ref, a_ref, b_ref)

    @pl.when(pl.program_id(0) == steps - 1)
    def _():
        tokens = m_ref.shape[0]
        lse = jnp.broadcast_to(all_ref[0, 0:1, :], (128, tokens)).T
        mean = jnp.broadcast_to(all_ref[0, 1:2, :], (128, tokens)).T
        own = jnp.exp(m_ref[...] - lse)
        ratio = own * (ce_weight + mean_ref[...] - mean)
        part = own[:, :1] * a_ref[...] + ratio[:, :1] * b_ref[...] - ce_weight * rows_ref[...]
        part_ref[...] = part.astype(part_ref.dtype)


def lat_specs(tokens, d, cb, first):
    return [
        pl.BlockSpec((tokens, d), lambda i: (0, 0)),
        pl.BlockSpec((tokens, d), lambda i: (0, 1)),
        pl.BlockSpec((tokens, 128), lambda i: (0, 0)),
        pl.BlockSpec((tokens, 128), lambda i: (0, 0)),
        pl.BlockSpec((cb, d), lambda i: (i + first, 0)),
    ]


def lat_first(toks, m_col, mean_col, book):
    tokens, (codes, d) = toks.shape[0], book.shape
    cb = 1024
    whole = pl.BlockSpec((tokens, d), lambda i: (0, 0))
    return pl.pallas_call(
        first_kernel,
        grid=(codes // cb // 2,),
        in_specs=lat_specs(tokens, d, cb, 0),
        out_specs=[whole] * 2,
        out_shape=[pltpu.HBM((tokens, d), F32)] * 2,
        compiler_params=params(),
        cost_estimate=cost(4 * tokens * codes * d, codes * d, tokens * codes // 2),
        name="lat_first",
    )(toks, toks, m_col, mean_col, book)


def lat_second(toks, m_col, mean_col, book, a, b, rows, row):
    tokens, (codes, d) = toks.shape[0], book.shape
    cb = 1024
    steps = codes // cb // 2
    whole = pl.BlockSpec((tokens, d), lambda i: (0, 0))
    return pl.pallas_call(
        functools.partial(second_kernel, steps),
        grid=(steps,),
        in_specs=lat_specs(tokens, d, cb, steps)
        + [whole] * 3
        + [pl.BlockSpec((1, 4, tokens), lambda i: (0, 0, 0))],
        out_specs=whole,
        out_shape=jax.ShapeDtypeStruct((tokens, d), BF16),
        scratch_shapes=[pltpu.VMEM((tokens, d), F32)] * 2,
        compiler_params=params(),
        cost_estimate=cost(4 * tokens * codes * d, codes * d, tokens * codes // 2),
        name="lat_second",
    )(toks, toks, m_col, mean_col, book, a, b, rows, row)


def combine_kernel(all_ref, tgt_ref, row_ref, loss_ref):
    stats = all_ref[...]
    m, l, w = stats[:, 0, :], stats[:, 1, :], stats[:, 2, :]
    top = jnp.max(m, axis=0, keepdims=True)
    scale = jnp.exp(m - top)
    total = jnp.sum(l * scale, axis=0, keepdims=True)
    mean = jnp.sum(w * scale, axis=0, keepdims=True) / total
    lse = top + jnp.log(total)
    pack = jnp.concatenate([lse, mean, tgt_ref[...].astype(F32), mean], axis=0)
    row_ref[...] = jnp.broadcast_to(pack[None], row_ref.shape)
    loss_ref[...] = lse - jnp.sum(stats[:, 3, :], axis=0, keepdims=True)


def combine(stats, tgt, groups):
    tokens = stats.shape[-1]
    return pl.pallas_call(
        combine_kernel,
        out_shape=[
            jax.ShapeDtypeStruct((groups, 4, tokens), F32),
            jax.ShapeDtypeStruct((1, tokens), F32),
        ],
        compiler_params=params(),
        cost_estimate=cost(tokens * 1000, tokens * 800),
        name="combine",
    )(stats, tgt)


def book_kernel(groups, s_ref, rows_ref, book_ref, *rest):
    toks, (out_ref, buf, sem) = rest[:groups], rest[groups:]
    for g in range(groups):
        pltpu.make_async_copy(toks[g], buf.at[g], sem.at[g]).start()
    block = book_ref[...]
    cb, d = block.shape
    out_ref[...] = jnp.zeros_like(out_ref)

    def step(g, carry):
        pltpu.make_async_copy(toks[0], buf.at[g], sem.at[g]).wait()
        row = rows_ref[s_ref[g]]
        tokens = row.shape[1]
        both = buf[g]
        lat, grad = both[:, :d], both[:, d:]
        logit = dot(block, lat, NT)
        back = dot(block, grad, NT)
        prob = jnp.exp(logit - row[0:1])
        ids = lax.broadcasted_iota(jnp.int32, (cb, tokens), 0)
        hit = jnp.where(ids == row[2:3].astype(jnp.int32) - s_ref[groups], 1.0, 0.0)
        delta = prob * (back - row[1:2]) + ce_weight * (prob - hit)
        out_ref[...] += dot(delta.astype(BF16), lat, NN) + dot(hit.astype(BF16), grad, NN)
        return carry

    lax.fori_loop(0, groups, step, 0)


def book_grad(scalars, rows, book, toks):
    groups = len(toks)
    (tokens, width), (chunk, d) = toks[0].shape, book.shape
    grid_spec = pltpu.PrefetchScalarGridSpec(
        num_scalar_prefetch=1,
        grid=(1,),
        in_specs=[
            pl.BlockSpec((groups, 4, tokens), lambda i, s: (0, 0, 0)),
            pl.BlockSpec((chunk, d), lambda i, s: (0, 0)),
        ]
        + [pl.BlockSpec(memory_space=pl.ANY)] * groups,
        out_specs=pl.BlockSpec((chunk, d), lambda i, s: (0, 0)),
        scratch_shapes=[
            pltpu.VMEM((groups, tokens, width), BF16),
            pltpu.SemaphoreType.DMA((groups,)),
        ],
    )
    return pl.pallas_call(
        functools.partial(book_kernel, groups),
        grid_spec=grid_spec,
        out_shape=jax.ShapeDtypeStruct((chunk, d), F32),
        compiler_params=params(),
        cost_estimate=cost(
            8 * groups * tokens * chunk * d, groups * tokens * width * 2, groups * tokens * chunk
        ),
        name="book_grad",
    )(scalars, rows, book, *toks)


def in_hbm(*arrays):
    return [pltpu.with_memory_space_constraint(x, pltpu.HBM) for x in arrays]


def per_device(latents, out_grad, targets, codebook):
    peers = lax.axis_size("z") * lax.axis_size("y")
    nx = lax.axis_size("x")
    own_count, d = latents.shape
    code_dev = codebook.shape[0]
    tokens = own_count * peers
    code_pos = lax.axis_index(ZY)
    x_pos, core = lax.axis_index("x"), lax.axis_index("core")
    dp_pos, chunk = x_pos * 2 + core, code_dev // (2 * nx)
    swap = [(0, 1), (1, 0)]
    book = pltpu.with_memory_space_constraint(codebook, pltpu.HBM)

    both = jnp.concatenate([latents, out_grad], axis=1)
    toks = lax.all_to_all(jnp.broadcast_to(both[None], (peers, own_count, 2 * d)), ZY, 0, 0)
    toks = toks.reshape(tokens, 2 * d)
    local_ids = targets - code_pos * code_dev
    rows = pick_rows(jnp.broadcast_to(local_ids[:, None], (tokens, 128)), book)
    (rows,) = in_hbm(rows)
    places = [lax.rem(x_pos + nx - k, nx) * 2 for k in range(nx)]
    scalars = [p + core for p in places] + [p + 1 - core for p in places]
    scalars += [code_pos * code_dev + dp_pos * chunk]
    scalars = jnp.stack(scalars).astype(jnp.int32)
    own_book = lax.dynamic_slice(codebook, (dp_pos * chunk, 0), (chunk, d))
    packed, m_col, mean_col = local_stats(toks, rows, book, peers)
    m_col, mean_col = in_hbm(m_col, mean_col)
    stats = lax.all_to_all(packed, ZY, 0, 0)
    late = lax.optimization_barrier((toks, packed))[0]
    same = [late]
    for k in range(1, nx):
        same.append(lax.ppermute(late, "x", [(i, (i + k) % nx) for i in range(nx)]))
    a, b = lat_first(toks, m_col, mean_col, book)
    row, loss = combine(stats, targets[None], 2 * nx)
    everyone = lax.all_to_all(row, XC, 0, 0)
    part = lat_second(toks, m_col, mean_col, book, *in_hbm(a, b), rows, row)
    part, everyone = lax.optimization_barrier((part, everyone))
    moved = lax.all_to_all(part.reshape(peers, own_count, d), ZY, 0, 0)
    latent_grad = jnp.sum(moved.astype(F32), axis=0).astype(BF16)
    token_loss = lax.dynamic_slice(loss, (0, code_pos * own_count), (1, own_count)).reshape(own_count)

    other = []
    for piece in same:
        other.append(lax.ppermute(piece, "core", swap))
    codebook_grad = book_grad(scalars, everyone, own_book, same + other)
    return latent_grad, codebook_grad, token_loss


def solution(mesh):
    shape = (mesh.shape["dp"] // 2, 2, mesh.shape["code"] // 4, 4)
    fine = Mesh(mesh.devices.reshape(shape), ("x", "core", "z", "y"))
    dp, code = ("x", "core"), ("z", "y")
    in_specs = (P(dp + code, None), P(dp + code, None), P(dp), P(code, None))
    out_specs = (P(dp + code, None), P(code + dp, None), P(dp + code))
    return jax.shard_map(
        per_device, mesh=fine, in_specs=in_specs, out_specs=out_specs, check_vma=False
    )
```

```python
import functools

import jax
import jax.numpy as jnp
from jax import lax
from jax.experimental import pallas as pl
from jax.experimental.pallas import tpu as pltpu
from jax.sharding import Mesh
from jax.sharding import PartitionSpec as P

ce_weight = 1.0
F32 = jnp.float32
BF16 = jnp.bfloat16
NT = (((1,), (1,)), ((), ()))
NN = (((1,), (0,)), ((), ()))
ZY = ("z", "y")
XC = ("x", "core")
VMEM_LIMIT = 32 << 20


def dot(a, b, dims, precision=None):
    return lax.dot_general(a, b, dims, preferred_element_type=F32, precision=precision)


def params(**kw):
    return pltpu.CompilerParams(vmem_limit_bytes=VMEM_LIMIT, **kw)


def cost(flops, bytes_accessed, trans=0):
    return pl.CostEstimate(flops=flops, bytes_accessed=bytes_accessed, transcendentals=trans)


def pick_kernel(cb, tgt_ref, book_ref, out_ref):
    i = pl.program_id(0)

    @pl.when(i == 0)
    def _():
        out_ref[...] = jnp.zeros_like(out_ref)

    tokens = tgt_ref.shape[0]
    ids = lax.broadcasted_iota(jnp.int32, (tokens, cb), 1) + i * cb
    hit = jnp.where(ids == tgt_ref[:, :1], 1.0, 0.0).astype(BF16)
    out_ref[...] += dot(hit, book_ref[...], NN)


def pick_rows(tgt_cols, book):
    tokens, codes, d = tgt_cols.shape[0], *book.shape
    cb = 2048
    return pl.pallas_call(
        functools.partial(pick_kernel, cb),
        grid=(codes // cb,),
        in_specs=[
            pl.BlockSpec((tokens, 128), lambda i: (0, 0)),
            pl.BlockSpec((cb, d), lambda i: (i, 0)),
        ],
        out_specs=pl.BlockSpec((tokens, d), lambda i: (0, 0)),
        out_shape=pltpu.HBM((tokens, d), F32),
        compiler_params=params(),
        cost_estimate=cost(2 * tokens * codes * d, codes * d * 2),
        name="pick",
    )(tgt_cols, book)


def fold(x):
    return sum(x[:, i : i + 128] for i in range(0, x.shape[1], 128))


def as_row(x):
    return jnp.sum(x.T, axis=0, keepdims=True)


def as_cols(row):
    return jnp.broadcast_to(row, (128, row.shape[1])).T


def stats_kernel(steps, sub, lat_ref, grad_ref, rows_ref, book_ref, out_ref, m_col, mean_col, m_s, l_s, w_s):
    i = pl.program_id(0)

    @pl.when(i == 0)
    def _():
        m_s[...] = jnp.full_like(m_s, -jnp.inf)
        l_s[...] = jnp.zeros_like(l_s)
        w_s[...] = jnp.zeros_like(w_s)

    cb, tokens = book_ref.shape[0], lat_ref.shape[0]
    count = cb // sub

    def scores(ref, j):
        return dot(book_ref[j * sub : (j + 1) * sub, :], ref[...], NT).reshape(sub // 8, 8, tokens)

    m, l, w = m_s[...], l_s[...], w_s[...]
    ahead = scores(lat_ref, 0)
    for j in range(count):
        logit = ahead
        if j + 1 < count:
            ahead = scores(lat_ref, j + 1)
        back = scores(grad_ref, j)
        new = jnp.maximum(m, jnp.max(logit, axis=0))
        factor = jnp.exp(m - new)
        expo = jnp.exp(logit - new[None])
        l = l * factor + jnp.sum(expo, axis=0)
        w = w * factor + jnp.sum(expo * back, axis=0)
        m = new
    m_s[...], l_s[...], w_s[...] = m, l, w

    @pl.when(i == steps - 1)
    def _():
        m = m_s[...]
        top = jnp.max(m, axis=0, keepdims=True)
        scale = jnp.exp(m - top)
        total = jnp.sum(l_s[...] * scale, axis=0, keepdims=True)
        weighted = jnp.sum(w_s[...] * scale, axis=0, keepdims=True)
        picked = as_row(fold(lat_ref[...].astype(F32) * rows_ref[...]))
        pack = jnp.concatenate([top, total, weighted, picked], axis=0)
        out_ref[...] = jnp.broadcast_to(pack[None], out_ref.shape)
        m_col[...] = as_cols(top)
        mean_col[...] = as_cols(weighted / total)


def local_stats(toks, rows, book, peers, cb=4096, sub=512):
    tokens, (codes, d) = toks.shape[0], book.shape
    steps = codes // cb
    cols = pl.BlockSpec((tokens, 128), lambda i: (0, 0))
    return pl.pallas_call(
        functools.partial(stats_kernel, steps, sub),
        grid=(steps,),
        in_specs=[
            pl.BlockSpec((tokens, d), lambda i: (0, 0)),
            pl.BlockSpec((tokens, d), lambda i: (0, 1)),
            pl.BlockSpec((tokens, d), lambda i: (0, 0)),
            pl.BlockSpec((cb, d), lambda i: (i, 0)),
        ],
        out_specs=[pl.BlockSpec((peers, 4, tokens), lambda i: (0, 0, 0)), cols, cols],
        out_shape=[
            jax.ShapeDtypeStruct((peers, 4, tokens), F32),
            pltpu.HBM((tokens, 128), F32),
            pltpu.HBM((tokens, 128), F32),
        ],
        scratch_shapes=[pltpu.VMEM((8, tokens), F32)] * 3,
        compiler_params=params(),
        cost_estimate=cost(4 * tokens * codes * d, codes * d * 2, tokens * codes),
        name="stats",
    )(toks, toks, rows, book)


def lat_step(sub, lat_ref, grad_ref, m_ref, book_ref, outs, weigh):
    count = book_ref.shape[0] // sub

    def block(j):
        return book_ref[j * sub : (j + 1) * sub, :]

    sums = [ref[...] for ref in outs]
    ahead = dot(lat_ref[...], block(0), NT)
    for j in range(count):
        logit = ahead
        if j + 1 < count:
            ahead = dot(lat_ref[...], block(j + 1), NT)
        back = dot(grad_ref[...], block(j), NT)
        terms = weigh(jnp.exp(logit - m_ref[:, :1]), back)
        sums = [x + dot(term.astype(BF16), block(j), NN) for x, term in zip(sums, terms)]
    for ref, x in zip(outs, sums):
        ref[...] = x


def first_kernel(sub, lat_ref, grad_ref, m_ref, mean_ref, book_ref, a_ref, b_ref):
    @pl.when(pl.program_id(0) == 0)
    def _():
        a_ref[...] = jnp.zeros_like(a_ref)
        b_ref[...] = jnp.zeros_like(b_ref)

    def weigh(expo, back):
        return expo * (back - mean_ref[:, :1]), expo

    lat_step(sub, lat_ref, grad_ref, m_ref, book_ref, (a_ref, b_ref), weigh)


def second_kernel(
    steps, sub, lat_ref, grad_ref, m_ref, mean_ref, book_ref, a0, b0, rows_ref, all_ref,
    part_ref, sum_ref, lse_col, mean_col,
):
    @pl.when(pl.program_id(0) == 0)
    def _():
        lse_col[...] = as_cols(all_ref[0, 0:1, :])
        mean_col[...] = as_cols(all_ref[0, 1:2, :])
        own = jnp.exp(m_ref[...] - lse_col[...])
        ratio = own * (ce_weight + mean_ref[...] - mean_col[...])
        sum_ref[...] = own[:, :1] * a0[...] + ratio[:, :1] * b0[...] - ce_weight * rows_ref[...]

    def weigh(prob, back):
        return (prob * (back - mean_col[:, :1]) + ce_weight * prob,)

    lat_step(sub, lat_ref, grad_ref, lse_col, book_ref, (sum_ref,), weigh)

    @pl.when(pl.program_id(0) == steps - 1)
    def _():
        part_ref[...] = sum_ref[...].astype(part_ref.dtype)


def lat_specs(tokens, d, cb, first):
    return [
        pl.BlockSpec((tokens, d), lambda i: (0, 0)),
        pl.BlockSpec((tokens, d), lambda i: (0, 1)),
        pl.BlockSpec((tokens, 128), lambda i: (0, 0)),
        pl.BlockSpec((tokens, 128), lambda i: (0, 0)),
        pl.BlockSpec((cb, d), lambda i: (i + first, 0)),
    ]


def lat_first(toks, m_col, mean_col, book, part=1, parts=2, cb=4096, sub=512):
    tokens, (codes, d) = toks.shape[0], book.shape
    steps = codes // cb * part // parts
    whole = pl.BlockSpec((tokens, d), lambda i: (0, 0))
    return pl.pallas_call(
        functools.partial(first_kernel, sub),
        grid=(steps,),
        in_specs=lat_specs(tokens, d, cb, 0),
        out_specs=[whole] * 2,
        out_shape=[pltpu.HBM((tokens, d), F32)] * 2,
        compiler_params=params(),
        cost_estimate=cost(8 * tokens * cb * steps * d, cb * steps * d * 2, tokens * cb * steps),
        name="lat_first",
    )(toks, toks, m_col, mean_col, book)


def lat_second(toks, m_col, mean_col, book, a, b, rows, row, part=1, parts=2, cb=4096, sub=512):
    tokens, (codes, d) = toks.shape[0], book.shape
    first = codes // cb * part // parts
    steps = codes // cb - first
    whole = pl.BlockSpec((tokens, d), lambda i: (0, 0))
    return pl.pallas_call(
        functools.partial(second_kernel, steps, sub),
        grid=(steps,),
        in_specs=lat_specs(tokens, d, cb, first)
        + [whole] * 3
        + [pl.BlockSpec((1, 4, tokens), lambda i: (0, 0, 0))],
        out_specs=whole,
        out_shape=jax.ShapeDtypeStruct((tokens, d), BF16),
        scratch_shapes=[pltpu.VMEM((tokens, d), F32)] + [pltpu.VMEM((tokens, 128), F32)] * 2,
        compiler_params=params(),
        cost_estimate=cost(6 * tokens * cb * steps * d, cb * steps * d * 2, tokens * cb * steps),
        name="lat_second",
    )(toks, toks, m_col, mean_col, book, a, b, rows, row)


def combine_kernel(all_ref, tgt_ref, row_ref, loss_ref):
    stats = all_ref[...]
    m, l, w = stats[:, 0, :], stats[:, 1, :], stats[:, 2, :]
    top = jnp.max(m, axis=0, keepdims=True)
    scale = jnp.exp(m - top)
    total = jnp.sum(l * scale, axis=0, keepdims=True)
    mean = jnp.sum(w * scale, axis=0, keepdims=True) / total
    lse = top + jnp.log(total)
    pack = jnp.concatenate([lse, mean, tgt_ref[...].astype(F32), mean], axis=0)
    row_ref[...] = jnp.broadcast_to(pack[None], row_ref.shape)
    loss_ref[...] = lse - jnp.sum(stats[:, 3, :], axis=0, keepdims=True)


def combine(stats, tgt, groups):
    tokens = stats.shape[-1]
    return pl.pallas_call(
        combine_kernel,
        out_shape=[
            jax.ShapeDtypeStruct((groups, 4, tokens), F32),
            jax.ShapeDtypeStruct((1, tokens), F32),
        ],
        compiler_params=params(),
        cost_estimate=cost(tokens * 1000, tokens * 800),
        name="combine",
    )(stats, tgt)


def book_kernel(first, sub, s_ref, rows_ref, book_ref, *rest):
    start, rest = (rest[:1], rest[1:]) if first else ((), rest)
    groups = len(rest) - 3
    toks, (out_ref, buf, sem) = rest[:groups], rest[groups:]
    for g in range(groups):
        pltpu.make_async_copy(toks[g], buf.at[g], sem.at[g]).start()
    chunk, d = book_ref.shape
    tokens = buf.shape[1]
    ids = lax.broadcasted_iota(jnp.int32, (sub, tokens), 0) + s_ref[s_ref.shape[0] - 1]
    work = [(g, j) for g in range(groups) for j in range(chunk // sub)]

    def block(j):
        return book_ref[j * sub : (j + 1) * sub, :]

    def logits(g, j):
        if j == 0:
            pltpu.make_async_copy(toks[g], buf.at[g], sem.at[g]).wait()
        return dot(block(j), buf[g, :, :d], NT)

    ahead = logits(*work[0])
    for n, (g, j) in enumerate(work):
        logit = ahead
        if n + 1 < len(work):
            ahead = logits(*work[n + 1])
        row = rows_ref[s_ref[first + g]]
        back = dot(block(j), buf[g, :, d:], NT)
        prob = jnp.exp(logit - row[0:1])
        hit = jnp.where(ids + j * sub == row[2:3].astype(jnp.int32), 1.0, 0.0)
        delta = prob * (back - row[1:2]) + ce_weight * (prob - hit)
        out = dot(delta.astype(BF16), buf[g, :, :d], NN) + dot(hit.astype(BF16), buf[g, :, d:], NN)
        at = slice(j * sub, (j + 1) * sub)
        if g == 0 and not start:
            out_ref[at, :] = out
        else:
            out_ref[at, :] = (start[0] if g == 0 else out_ref)[at, :] + out


def book_grad(scalars, rows, book, toks, start=None, sub=512):
    groups = len(toks)
    (tokens, width), (chunk, d) = toks[0].shape, book.shape
    whole = pl.BlockSpec((chunk, d), lambda i, s: (0, 0))
    extra = [] if start is None else [start]
    grid_spec = pltpu.PrefetchScalarGridSpec(
        num_scalar_prefetch=1,
        grid=(1,),
        in_specs=[pl.BlockSpec(rows.shape, lambda i, s: (0, 0, 0)), whole]
        + [whole for _ in extra]
        + [pl.BlockSpec(memory_space=pl.ANY)] * groups,
        out_specs=whole,
        scratch_shapes=[
            pltpu.VMEM((groups, tokens, width), BF16),
            pltpu.SemaphoreType.DMA((groups,)),
        ],
    )
    return pl.pallas_call(
        functools.partial(book_kernel, 0 if start is None else groups, sub),
        grid_spec=grid_spec,
        out_shape=jax.ShapeDtypeStruct((chunk, d), F32),
        compiler_params=params(),
        cost_estimate=cost(
            8 * groups * tokens * chunk * d, groups * tokens * width * 2, groups * tokens * chunk
        ),
        name="book_first" if start is None else "book_second",
    )(scalars, rows, book, *extra, *toks)


def in_hbm(*arrays):
    return [pltpu.with_memory_space_constraint(x, pltpu.HBM) for x in arrays]


def per_device(latents, out_grad, targets, codebook):
    peers = lax.axis_size("z") * lax.axis_size("y")
    nx = lax.axis_size("x")
    own_count, d = latents.shape
    code_dev = codebook.shape[0]
    tokens = own_count * peers
    code_pos = lax.axis_index(ZY)
    x_pos, core = lax.axis_index("x"), lax.axis_index("core")
    dp_pos, chunk = x_pos * 2 + core, code_dev // (2 * nx)
    swap = [(0, 1), (1, 0)]
    book = pltpu.with_memory_space_constraint(codebook, pltpu.HBM)

    both = jnp.concatenate([latents, out_grad], axis=1)
    toks = lax.all_to_all(jnp.broadcast_to(both[None], (peers, own_count, 2 * d)), ZY, 0, 0)
    toks = toks.reshape(tokens, 2 * d)
    local_ids = targets - code_pos * code_dev
    rows = pick_rows(jnp.broadcast_to(local_ids[:, None], (tokens, 128)), book)
    (rows,) = in_hbm(rows)
    places = [lax.rem(x_pos + nx - k, nx) * 2 for k in range(nx)]
    scalars = [p + core for p in places] + [p + 1 - core for p in places]
    scalars += [code_pos * code_dev + dp_pos * chunk]
    scalars = jnp.stack(scalars).astype(jnp.int32)
    own_book = lax.dynamic_slice(codebook, (dp_pos * chunk, 0), (chunk, d))
    packed, m_col, mean_col = local_stats(toks, rows, book, peers)
    m_col, mean_col = in_hbm(m_col, mean_col)
    stats = lax.all_to_all(packed, ZY, 0, 0)
    late = lax.optimization_barrier((toks, packed))[0]
    same = [late]
    for k in range(1, nx):
        same.append(lax.ppermute(late, "x", [(i, (i + k) % nx) for i in range(nx)]))
    a, b = lat_first(toks, m_col, mean_col, book)
    row, loss = combine(stats, targets[None], 2 * nx)
    everyone = lax.all_to_all(row, XC, 0, 0)
    part = lat_second(toks, m_col, mean_col, book, *in_hbm(a, b), rows, row)
    part, everyone = lax.optimization_barrier((part, everyone))
    moved = lax.all_to_all(part.reshape(peers, own_count, d), ZY, 0, 0)
    latent_grad = jnp.sum(moved.astype(F32), axis=0).astype(BF16)
    token_loss = lax.dynamic_slice(loss, (0, code_pos * own_count), (1, own_count)).reshape(own_count)

    other = []
    for piece in same:
        other.append(lax.ppermute(piece, "core", swap))
    half = book_grad(scalars, everyone, own_book, same)
    codebook_grad = book_grad(scalars, everyone, own_book, other, half)
    return latent_grad, codebook_grad, token_loss


def solution(mesh):
    shape = (mesh.shape["dp"] // 2, 2, mesh.shape["code"] // 4, 4)
    fine = Mesh(mesh.devices.reshape(shape), ("x", "core", "z", "y"))
    dp, code = ("x", "core"), ("z", "y")
    in_specs = (P(dp + code, None), P(dp + code, None), P(dp), P(code, None))
    out_specs = (P(dp + code, None), P(code + dp, None), P(dp + code))
    return jax.shard_map(
        per_device, mesh=fine, in_specs=in_specs, out_specs=out_specs, check_vma=False
    )
```

```python
import functools

import jax
import jax.numpy as jnp
from jax import lax
from jax.experimental import pallas as pl
from jax.experimental.pallas import tpu as pltpu
from jax.sharding import Mesh
from jax.sharding import PartitionSpec as P

ce_weight = 1.0
F32 = jnp.float32
BF16 = jnp.bfloat16
NT = (((1,), (1,)), ((), ()))
NN = (((1,), (0,)), ((), ()))
ZY = ("z", "y")
XC = ("x", "core")
VMEM_LIMIT = 32 << 20


def dot(a, b, dims, precision=None):
    return lax.dot_general(a, b, dims, preferred_element_type=F32, precision=precision)


def params(**kw):
    return pltpu.CompilerParams(vmem_limit_bytes=VMEM_LIMIT, **kw)


def cost(flops, bytes_accessed, trans=0):
    return pl.CostEstimate(flops=flops, bytes_accessed=bytes_accessed, transcendentals=trans)


def pick_kernel(cb, tgt_ref, book_ref, out_ref):
    i = pl.program_id(0)

    @pl.when(i == 0)
    def _():
        out_ref[...] = jnp.zeros_like(out_ref)

    tokens = tgt_ref.shape[0]
    ids = lax.broadcasted_iota(jnp.int32, (tokens, cb), 1) + i * cb
    hit = jnp.where(ids == tgt_ref[:, :1], 1.0, 0.0).astype(BF16)
    out_ref[...] += dot(hit, book_ref[...], NN)


def pick_rows(tgt_cols, book):
    tokens, codes, d = tgt_cols.shape[0], *book.shape
    cb = 2048
    return pl.pallas_call(
        functools.partial(pick_kernel, cb),
        grid=(codes // cb,),
        in_specs=[
            pl.BlockSpec((tokens, 128), lambda i: (0, 0)),
            pl.BlockSpec((cb, d), lambda i: (i, 0)),
        ],
        out_specs=pl.BlockSpec((tokens, d), lambda i: (0, 0)),
        out_shape=pltpu.HBM((tokens, d), F32),
        compiler_params=params(),
        cost_estimate=cost(2 * tokens * codes * d, codes * d * 2),
        name="pick",
    )(tgt_cols, book)


def fold(x):
    return sum(x[:, i : i + 128] for i in range(0, x.shape[1], 128))


def as_row(x):
    return jnp.sum(x.T, axis=0, keepdims=True)


def as_cols(row):
    return jnp.broadcast_to(row, (128, row.shape[1])).T


def stats_kernel(steps, sub, lat_ref, grad_ref, rows_ref, book_ref, out_ref, m_col, mean_col, m_s, l_s, w_s):
    i = pl.program_id(0)

    @pl.when(i == 0)
    def _():
        m_s[...] = jnp.full_like(m_s, -jnp.inf)
        l_s[...] = jnp.zeros_like(l_s)
        w_s[...] = jnp.zeros_like(w_s)

    cb, tokens = book_ref.shape[0], lat_ref.shape[0]
    count = cb // sub

    def scores(ref, j):
        return dot(book_ref[j * sub : (j + 1) * sub, :], ref[...], NT).reshape(sub // 8, 8, tokens)

    m, l, w = m_s[...], l_s[...], w_s[...]
    ahead = scores(lat_ref, 0)
    for j in range(count):
        logit = ahead
        if j + 1 < count:
            ahead = scores(lat_ref, j + 1)
        back = scores(grad_ref, j)
        new = jnp.maximum(m, jnp.max(logit, axis=0))
        factor = jnp.exp(m - new)
        expo = jnp.exp(logit - new[None])
        l = l * factor + jnp.sum(expo, axis=0)
        w = w * factor + jnp.sum(expo * back, axis=0)
        m = new
    m_s[...], l_s[...], w_s[...] = m, l, w

    @pl.when(i == steps - 1)
    def _():
        m = m_s[...]
        top = jnp.max(m, axis=0, keepdims=True)
        scale = jnp.exp(m - top)
        total = jnp.sum(l_s[...] * scale, axis=0, keepdims=True)
        weighted = jnp.sum(w_s[...] * scale, axis=0, keepdims=True)
        picked = as_row(fold(lat_ref[...].astype(F32) * rows_ref[...]))
        pack = jnp.concatenate([top, total, weighted, picked], axis=0)
        out_ref[...] = jnp.broadcast_to(pack[None], out_ref.shape)
        m_col[...] = as_cols(top)
        mean_col[...] = as_cols(weighted / total)


def local_stats(toks, rows, book, peers, cb=2048, sub=512):
    tokens, (codes, d) = toks.shape[0], book.shape
    steps = codes // cb
    cols = pl.BlockSpec((tokens, 128), lambda i: (0, 0))
    return pl.pallas_call(
        functools.partial(stats_kernel, steps, sub),
        grid=(steps,),
        in_specs=[
            pl.BlockSpec((tokens, d), lambda i: (0, 0)),
            pl.BlockSpec((tokens, d), lambda i: (0, 1)),
            pl.BlockSpec((tokens, d), lambda i: (0, 0)),
            pl.BlockSpec((cb, d), lambda i: (i, 0)),
        ],
        out_specs=[pl.BlockSpec((peers, 4, tokens), lambda i: (0, 0, 0)), cols, cols],
        out_shape=[
            jax.ShapeDtypeStruct((peers, 4, tokens), F32),
            pltpu.HBM((tokens, 128), F32),
            pltpu.HBM((tokens, 128), F32),
        ],
        scratch_shapes=[pltpu.VMEM((8, tokens), F32)] * 3,
        compiler_params=params(),
        cost_estimate=cost(4 * tokens * codes * d, codes * d * 2, tokens * codes),
        name="stats",
    )(toks, toks, rows, book)


def lat_step(sub, lat_ref, grad_ref, m_ref, book_ref, outs, weigh):
    count = book_ref.shape[0] // sub

    def block(j):
        return book_ref[j * sub : (j + 1) * sub, :]

    sums = [ref[...] for ref in outs]
    ahead = dot(lat_ref[...], block(0), NT)
    for j in range(count):
        logit = ahead
        if j + 1 < count:
            ahead = dot(lat_ref[...], block(j + 1), NT)
        back = dot(grad_ref[...], block(j), NT)
        terms = weigh(jnp.exp(logit - m_ref[:, :1]), back)
        sums = [x + dot(term.astype(BF16), block(j), NN) for x, term in zip(sums, terms)]
    for ref, x in zip(outs, sums):
        ref[...] = x


def first_kernel(sub, lat_ref, grad_ref, m_ref, mean_ref, book_ref, a_ref, b_ref):
    @pl.when(pl.program_id(0) == 0)
    def _():
        a_ref[...] = jnp.zeros_like(a_ref)
        b_ref[...] = jnp.zeros_like(b_ref)

    def weigh(expo, back):
        return expo * (back - mean_ref[:, :1]), expo

    lat_step(sub, lat_ref, grad_ref, m_ref, book_ref, (a_ref, b_ref), weigh)


def second_kernel(
    steps, sub, lat_ref, grad_ref, m_ref, mean_ref, book_ref, a0, b0, rows_ref, all_ref,
    part_ref, sum_ref, lse_col, mean_col,
):
    @pl.when(pl.program_id(0) == 0)
    def _():
        lse_col[...] = as_cols(all_ref[0, 0:1, :])
        mean_col[...] = as_cols(all_ref[0, 1:2, :])
        own = jnp.exp(m_ref[...] - lse_col[...])
        ratio = own * (ce_weight + mean_ref[...] - mean_col[...])
        sum_ref[...] = own[:, :1] * a0[...] + ratio[:, :1] * b0[...] - ce_weight * rows_ref[...]

    def weigh(prob, back):
        return (prob * (back - mean_col[:, :1]) + ce_weight * prob,)

    lat_step(sub, lat_ref, grad_ref, lse_col, book_ref, (sum_ref,), weigh)

    @pl.when(pl.program_id(0) == steps - 1)
    def _():
        part_ref[...] = sum_ref[...].astype(part_ref.dtype)


def lat_specs(tokens, d, cb, first):
    return [
        pl.BlockSpec((tokens, d), lambda i: (0, 0)),
        pl.BlockSpec((tokens, d), lambda i: (0, 1)),
        pl.BlockSpec((tokens, 128), lambda i: (0, 0)),
        pl.BlockSpec((tokens, 128), lambda i: (0, 0)),
        pl.BlockSpec((cb, d), lambda i: (i + first, 0)),
    ]


def lat_first(toks, m_col, mean_col, book, part=1, parts=2, cb=2048, sub=512):
    tokens, (codes, d) = toks.shape[0], book.shape
    steps = codes // cb * part // parts
    whole = pl.BlockSpec((tokens, d), lambda i: (0, 0))
    return pl.pallas_call(
        functools.partial(first_kernel, sub),
        grid=(steps,),
        in_specs=lat_specs(tokens, d, cb, 0),
        out_specs=[whole] * 2,
        out_shape=[pltpu.HBM((tokens, d), F32)] * 2,
        compiler_params=params(),
        cost_estimate=cost(8 * tokens * cb * steps * d, cb * steps * d * 2, tokens * cb * steps),
        name="lat_first",
    )(toks, toks, m_col, mean_col, book)


def lat_second(toks, m_col, mean_col, book, a, b, rows, row, part=1, parts=2, cb=2048, sub=512):
    tokens, (codes, d) = toks.shape[0], book.shape
    first = codes // cb * part // parts
    steps = codes // cb - first
    whole = pl.BlockSpec((tokens, d), lambda i: (0, 0))
    return pl.pallas_call(
        functools.partial(second_kernel, steps, sub),
        grid=(steps,),
        in_specs=lat_specs(tokens, d, cb, first)
        + [whole] * 3
        + [pl.BlockSpec((1, 4, tokens), lambda i: (0, 0, 0))],
        out_specs=whole,
        out_shape=jax.ShapeDtypeStruct((tokens, d), BF16),
        scratch_shapes=[pltpu.VMEM((tokens, d), F32)] + [pltpu.VMEM((tokens, 128), F32)] * 2,
        compiler_params=params(),
        cost_estimate=cost(6 * tokens * cb * steps * d, cb * steps * d * 2, tokens * cb * steps),
        name="lat_second",
    )(toks, toks, m_col, mean_col, book, a, b, rows, row)


def combine_kernel(all_ref, tgt_ref, first_ref, row_ref, loss_ref):
    stats = all_ref[...]
    m, l, w = stats[:, 0, :], stats[:, 1, :], stats[:, 2, :]
    tokens = m.shape[1]
    top = jnp.max(m, axis=0, keepdims=True)
    scale = jnp.exp(m - top)
    total = jnp.sum(l * scale, axis=0, keepdims=True)
    mean = jnp.sum(w * scale, axis=0, keepdims=True) / total
    lse = top + jnp.log(total)
    pack = jnp.concatenate([lse, mean, tgt_ref[...].astype(F32), mean], axis=0)
    row_ref[...] = jnp.broadcast_to(pack[None], row_ref.shape)
    loss = jnp.broadcast_to(lse - jnp.sum(stats[:, 3, :], axis=0, keepdims=True), (8, tokens))
    loss_ref[...] = pltpu.roll(loss, first_ref[0], 1)[:1, : loss_ref.shape[1]]


def combine(stats, tgt, first, groups, count):
    tokens = stats.shape[-1]
    vmem = pl.BlockSpec(memory_space=pltpu.VMEM)
    return pl.pallas_call(
        combine_kernel,
        in_specs=[vmem, vmem, pl.BlockSpec(memory_space=pltpu.SMEM)],
        out_shape=[
            jax.ShapeDtypeStruct((groups, 4, tokens), F32),
            jax.ShapeDtypeStruct((1, count), F32),
        ],
        compiler_params=params(),
        cost_estimate=cost(tokens * 1000, tokens * 800),
        name="combine",
    )(stats, tgt, first)


def book_kernel(sub, batch, s_ref, rows_ref, book_ref, *rest):
    groups = len(rest) - 3
    toks, (out_ref, buf, sem) = rest[:groups], rest[groups:]
    for g in range(groups):
        pltpu.make_async_copy(toks[g], buf.at[g], sem.at[g]).start()
    chunk, d = book_ref.shape
    tokens = buf.shape[1]
    ids = lax.broadcasted_iota(jnp.int32, (sub, tokens), 0) + s_ref[groups]
    out_ref[...] = jnp.zeros_like(out_ref)

    def block(j):
        return book_ref[j * sub : (j + 1) * sub, :]

    def step(i, carry):
        work = [(i * batch + k, j) for k in range(batch) for j in range(chunk // sub)]

        def logits(g, j):
            if j == 0:
                pltpu.make_async_copy(toks[0], buf.at[g], sem.at[g]).wait()
            return dot(block(j), buf[g, :, :d], NT)

        ahead = logits(*work[0])
        for n, (g, j) in enumerate(work):
            logit = ahead
            if n + 1 < len(work):
                ahead = logits(*work[n + 1])
            row = rows_ref[s_ref[g]]
            back = dot(block(j), buf[g, :, d:], NT)
            prob = jnp.exp(logit - row[0:1])
            hit = jnp.where(ids + j * sub == row[2:3].astype(jnp.int32), 1.0, 0.0)
            delta = prob * (back - row[1:2]) + ce_weight * (prob - hit)
            at = slice(j * sub, (j + 1) * sub)
            out_ref[at, :] += dot(delta.astype(BF16), buf[g, :, :d], NN) + dot(
                hit.astype(BF16), buf[g, :, d:], NN
            )
        return carry

    lax.fori_loop(0, groups // batch, step, 0)


def book_grad(scalars, rows, book, toks, sub=512, batch=1):
    groups = len(toks)
    (tokens, width), (chunk, d) = toks[0].shape, book.shape
    whole = pl.BlockSpec((chunk, d), lambda i, s: (0, 0))
    grid_spec = pltpu.PrefetchScalarGridSpec(
        num_scalar_prefetch=1,
        grid=(1,),
        in_specs=[pl.BlockSpec(rows.shape, lambda i, s: (0, 0, 0)), whole]
        + [pl.BlockSpec(memory_space=pl.ANY)] * groups,
        out_specs=whole,
        scratch_shapes=[
            pltpu.VMEM((groups, tokens, width), BF16),
            pltpu.SemaphoreType.DMA((groups,)),
        ],
    )
    return pl.pallas_call(
        functools.partial(book_kernel, sub, batch),
        grid_spec=grid_spec,
        out_shape=jax.ShapeDtypeStruct((chunk, d), F32),
        compiler_params=params(),
        cost_estimate=cost(
            8 * groups * tokens * chunk * d, groups * tokens * width * 2, groups * tokens * chunk
        ),
        name="book_grad",
    )(scalars, rows, book, *toks)


def spread_kernel(lat_ref, grad_ref, out_ref):
    both = jnp.concatenate([lat_ref[...], grad_ref[...]], axis=1)
    out_ref[...] = jnp.broadcast_to(both[None], out_ref.shape)


def spread(lat, grad, peers):
    count, d = lat.shape
    return pl.pallas_call(
        spread_kernel,
        out_shape=jax.ShapeDtypeStruct((peers, count, 2 * d), BF16),
        compiler_params=params(),
        name="spread",
    )(lat, grad)


def gather_kernel(in_ref, out_ref):
    out_ref[...] = jnp.sum(in_ref[...].astype(F32), axis=0).astype(out_ref.dtype)


def sum_parts(parts):
    return pl.pallas_call(
        gather_kernel,
        out_shape=jax.ShapeDtypeStruct(parts.shape[1:], BF16),
        compiler_params=params(),
        name="sum_parts",
    )(parts)


def in_hbm(*arrays):
    return [pltpu.with_memory_space_constraint(x, pltpu.HBM) for x in arrays]


def per_device(latents, out_grad, targets, codebook):
    peers = lax.axis_size("z") * lax.axis_size("y")
    nx = lax.axis_size("x")
    own_count, d = latents.shape
    code_dev = codebook.shape[0]
    tokens = own_count * peers
    code_pos = lax.axis_index(ZY)
    x_pos, core = lax.axis_index("x"), lax.axis_index("core")
    dp_pos, chunk = x_pos * 2 + core, code_dev // (2 * nx)
    swap = [(0, 1), (1, 0)]
    book = pltpu.with_memory_space_constraint(codebook, pltpu.HBM)

    toks = lax.all_to_all(spread(*in_hbm(latents, out_grad), peers), ZY, 0, 0)
    toks = toks.reshape(tokens, 2 * d)
    local_ids = targets - code_pos * code_dev
    rows = pick_rows(jnp.broadcast_to(local_ids[:, None], (tokens, 128)), book)
    (rows,) = in_hbm(rows)
    places = [lax.rem(x_pos + nx - k, nx) * 2 for k in range(nx)]
    scalars = [p + core for p in places] + [p + 1 - core for p in places]
    scalars += [code_pos * code_dev + dp_pos * chunk]
    scalars = jnp.stack(scalars).astype(jnp.int32)
    own_book = lax.dynamic_slice(codebook, (dp_pos * chunk, 0), (chunk, d))
    packed, m_col, mean_col = local_stats(toks, rows, book, peers)
    m_col, mean_col = in_hbm(m_col, mean_col)
    stats = lax.all_to_all(packed, ZY, 0, 0)
    same = [toks]
    for k in range(1, nx):
        same.append(lax.ppermute(toks, "x", [(i, (i + k) % nx) for i in range(nx)]))
    a, b = lat_first(toks, m_col, mean_col, book)
    shift = lax.rem(tokens - code_pos * own_count, tokens).astype(jnp.int32).reshape(1)
    row, loss = combine(stats, targets[None], shift, 2 * nx, own_count)
    everyone = lax.all_to_all(row, XC, 0, 0)
    part = lat_second(toks, m_col, mean_col, book, *in_hbm(a, b), rows, row)
    part, everyone = lax.optimization_barrier((part, everyone))
    moved = lax.all_to_all(part.reshape(peers, own_count, d), ZY, 0, 0)
    latent_grad = sum_parts(moved)
    token_loss = loss.reshape(own_count)

    other = []
    for piece in same:
        other.append(lax.ppermute(piece, "core", swap))
    codebook_grad = book_grad(scalars, everyone, own_book, same + other)
    return latent_grad, codebook_grad, token_loss


def solution(mesh):
    shape = (mesh.shape["dp"] // 2, 2, mesh.shape["code"] // 4, 4)
    fine = Mesh(mesh.devices.reshape(shape), ("x", "core", "z", "y"))
    dp, code = ("x", "core"), ("z", "y")
    in_specs = (P(dp + code, None), P(dp + code, None), P(dp), P(code, None))
    out_specs = (P(dp + code, None), P(code + dp, None), P(dp + code))
    return jax.shard_map(
        per_device, mesh=fine, in_specs=in_specs, out_specs=out_specs, check_vma=False
    )
```

```python
import functools

import jax
import jax.numpy as jnp
from jax import lax
from jax.experimental import pallas as pl
from jax.experimental.pallas import tpu as pltpu
from jax.sharding import Mesh
from jax.sharding import PartitionSpec as P

ce_weight = 1.0
F32 = jnp.float32
BF16 = jnp.bfloat16
NT = (((1,), (1,)), ((), ()))
NN = (((1,), (0,)), ((), ()))
ZY = ("z", "y")
XC = ("x", "core")
VMEM_LIMIT = 32 << 20


def dot(a, b, dims, precision=None):
    return lax.dot_general(a, b, dims, preferred_element_type=F32, precision=precision)


def params(**kw):
    return pltpu.CompilerParams(vmem_limit_bytes=VMEM_LIMIT, **kw)


def cost(flops, bytes_accessed, trans=0):
    return pl.CostEstimate(flops=flops, bytes_accessed=bytes_accessed, transcendentals=trans)


def pick_kernel(cb, tgt_ref, book_ref, out_ref):
    i = pl.program_id(0)

    @pl.when(i == 0)
    def _():
        out_ref[...] = jnp.zeros_like(out_ref)

    tokens = tgt_ref.shape[0]
    ids = lax.broadcasted_iota(jnp.int32, (tokens, cb), 1) + i * cb
    hit = jnp.where(ids == tgt_ref[:, :1], 1.0, 0.0).astype(BF16)
    out_ref[...] += dot(hit, book_ref[...], NN)


def pick_rows(tgt_cols, book):
    tokens, codes, d = tgt_cols.shape[0], *book.shape
    cb = 2048
    return pl.pallas_call(
        functools.partial(pick_kernel, cb),
        grid=(codes // cb,),
        in_specs=[
            pl.BlockSpec((tokens, 128), lambda i: (0, 0)),
            pl.BlockSpec((cb, d), lambda i: (i, 0)),
        ],
        out_specs=pl.BlockSpec((tokens, d), lambda i: (0, 0)),
        out_shape=pltpu.HBM((tokens, d), F32),
        compiler_params=params(),
        cost_estimate=cost(2 * tokens * codes * d, codes * d * 2),
        name="pick",
    )(tgt_cols, book)


def fold(x):
    return sum(x[:, i : i + 128] for i in range(0, x.shape[1], 128))


def as_row(x):
    return jnp.sum(x.T, axis=0, keepdims=True)


def as_cols(row):
    return jnp.broadcast_to(row, (128, row.shape[1])).T


def stats_kernel(
    steps, sub, lat_ref, grad_ref, book_ref, rows_hbm, out_ref, m_col, mean_col, m_s, l_s, w_s, rows_ref, sem
):
    i = pl.program_id(0)
    load = pltpu.make_async_copy(rows_hbm, rows_ref, sem)

    @pl.when(i == 0)
    def _():
        load.start()
        m_s[...] = jnp.full_like(m_s, -jnp.inf)
        l_s[...] = jnp.zeros_like(l_s)
        w_s[...] = jnp.zeros_like(w_s)

    cb, tokens = book_ref.shape[0], lat_ref.shape[0]
    count = cb // sub

    def scores(ref, j):
        return dot(book_ref[j * sub : (j + 1) * sub, :], ref[...], NT).reshape(sub // 8, 8, tokens)

    m, l, w = m_s[...], l_s[...], w_s[...]
    ahead = scores(lat_ref, 0)
    for j in range(count):
        logit = ahead
        if j + 1 < count:
            ahead = scores(lat_ref, j + 1)
        back = scores(grad_ref, j)
        new = jnp.maximum(m, jnp.max(logit, axis=0))
        factor = jnp.exp(m - new)
        expo = jnp.exp(logit - new[None])
        l = l * factor + jnp.sum(expo, axis=0)
        w = w * factor + jnp.sum(expo * back, axis=0)
        m = new
    m_s[...], l_s[...], w_s[...] = m, l, w

    @pl.when(i == steps - 1)
    def _():
        m = m_s[...]
        top = jnp.max(m, axis=0, keepdims=True)
        scale = jnp.exp(m - top)
        total = jnp.sum(l_s[...] * scale, axis=0, keepdims=True)
        weighted = jnp.sum(w_s[...] * scale, axis=0, keepdims=True)
        load.wait()
        picked = as_row(fold(lat_ref[...].astype(F32) * rows_ref[...]))
        pack = jnp.concatenate([top, total, weighted, picked], axis=0)
        out_ref[...] = jnp.broadcast_to(pack[None], out_ref.shape)
        m_col[...] = as_cols(top)
        mean_col[...] = as_cols(weighted / total)


def local_stats(toks, rows, book, peers, cb=2048, sub=512):
    tokens, (codes, d) = toks.shape[0], book.shape
    steps = codes // cb
    cols = pl.BlockSpec((tokens, 128), lambda i: (0, 0))
    return pl.pallas_call(
        functools.partial(stats_kernel, steps, sub),
        grid=(steps,),
        in_specs=[
            pl.BlockSpec((tokens, d), lambda i: (0, 0)),
            pl.BlockSpec((tokens, d), lambda i: (0, 1)),
            pl.BlockSpec((cb, d), lambda i: (i, 0)),
            pl.BlockSpec(memory_space=pltpu.HBM),
        ],
        out_specs=[pl.BlockSpec((peers, 4, tokens), lambda i: (0, 0, 0)), cols, cols],
        out_shape=[
            jax.ShapeDtypeStruct((peers, 4, tokens), F32),
            pltpu.HBM((tokens, 128), F32),
            pltpu.HBM((tokens, 128), F32),
        ],
        scratch_shapes=[pltpu.VMEM((8, tokens), F32)] * 3
        + [pltpu.VMEM((tokens, d), F32), pltpu.SemaphoreType.DMA],
        compiler_params=params(),
        cost_estimate=cost(4 * tokens * codes * d, codes * d * 2, tokens * codes),
        name="stats",
    )(toks, toks, book, rows)


def lat_step(sub, lat_ref, grad_ref, m_ref, book_ref, outs, weigh):
    count = book_ref.shape[0] // sub

    def block(j):
        return book_ref[j * sub : (j + 1) * sub, :]

    sums = [ref[...] for ref in outs]
    ahead = dot(lat_ref[...], block(0), NT)
    for j in range(count):
        logit = ahead
        if j + 1 < count:
            ahead = dot(lat_ref[...], block(j + 1), NT)
        back = dot(grad_ref[...], block(j), NT)
        terms = weigh(jnp.exp(logit - m_ref[:, :1]), back)
        sums = [x + dot(term.astype(BF16), block(j), NN) for x, term in zip(sums, terms)]
    for ref, x in zip(outs, sums):
        ref[...] = x


def first_kernel(sub, lat_ref, grad_ref, m_ref, mean_ref, book_ref, a_ref, b_ref):
    @pl.when(pl.program_id(0) == 0)
    def _():
        a_ref[...] = jnp.zeros_like(a_ref)
        b_ref[...] = jnp.zeros_like(b_ref)

    def weigh(expo, back):
        return expo * (back - mean_ref[:, :1]), expo

    lat_step(sub, lat_ref, grad_ref, m_ref, book_ref, (a_ref, b_ref), weigh)


def second_kernel(
    steps, sub, lat_ref, grad_ref, book_ref, all_ref, m_hbm, mean_hbm, a_hbm, b_hbm, rows_hbm,
    part_ref, sum_ref, lse_col, mean_col, m_ref, own_mean, a_ref, b_ref, rows_ref, sem,
):
    i = pl.program_id(0)
    pairs = ((m_hbm, m_ref), (mean_hbm, own_mean), (a_hbm, a_ref), (b_hbm, b_ref), (rows_hbm, rows_ref))
    loads = [pltpu.make_async_copy(src, dst, sem.at[n]) for n, (src, dst) in enumerate(pairs)]

    @pl.when(i == 0)
    def _():
        for load in loads:
            load.start()
        lse_col[...] = as_cols(all_ref[0, 0:1, :])
        mean_col[...] = as_cols(all_ref[0, 1:2, :])
        sum_ref[...] = jnp.zeros_like(sum_ref)

    def weigh(prob, back):
        return (prob * (back - mean_col[:, :1]) + ce_weight * prob,)

    lat_step(sub, lat_ref, grad_ref, lse_col, book_ref, (sum_ref,), weigh)

    @pl.when(i == steps - 1)
    def _():
        for load in loads:
            load.wait()
        own = jnp.exp(m_ref[...] - lse_col[...])
        ratio = own * (ce_weight + own_mean[...] - mean_col[...])
        part = own[:, :1] * a_ref[...] + ratio[:, :1] * b_ref[...] - ce_weight * rows_ref[...]
        part_ref[...] = (sum_ref[...] + part).astype(part_ref.dtype)


def lat_specs(tokens, d, cb, first):
    return [
        pl.BlockSpec((tokens, d), lambda i: (0, 0)),
        pl.BlockSpec((tokens, d), lambda i: (0, 1)),
        pl.BlockSpec((tokens, 128), lambda i: (0, 0)),
        pl.BlockSpec((tokens, 128), lambda i: (0, 0)),
        pl.BlockSpec((cb, d), lambda i: (i + first, 0)),
    ]


def lat_first(toks, m_col, mean_col, book, part=1, parts=2, cb=2048, sub=512):
    tokens, (codes, d) = toks.shape[0], book.shape
    steps = codes // cb * part // parts
    whole = pl.BlockSpec((tokens, d), lambda i: (0, 0))
    return pl.pallas_call(
        functools.partial(first_kernel, sub),
        grid=(steps,),
        in_specs=lat_specs(tokens, d, cb, 0),
        out_specs=[whole] * 2,
        out_shape=[pltpu.HBM((tokens, d), F32)] * 2,
        compiler_params=params(),
        cost_estimate=cost(8 * tokens * cb * steps * d, cb * steps * d * 2, tokens * cb * steps),
        name="lat_first",
    )(toks, toks, m_col, mean_col, book)


def lat_second(toks, m_col, mean_col, book, a, b, rows, row, part=1, parts=2, cb=2048, sub=512):
    tokens, (codes, d) = toks.shape[0], book.shape
    first = codes // cb * part // parts
    steps = codes // cb - first
    whole = pl.BlockSpec((tokens, d), lambda i: (0, 0))
    return pl.pallas_call(
        functools.partial(second_kernel, steps, sub),
        grid=(steps,),
        in_specs=[
            pl.BlockSpec((tokens, d), lambda i: (0, 0)),
            pl.BlockSpec((tokens, d), lambda i: (0, 1)),
            pl.BlockSpec((cb, d), lambda i: (i + first, 0)),
            pl.BlockSpec((1, 4, tokens), lambda i: (0, 0, 0)),
        ]
        + [pl.BlockSpec(memory_space=pltpu.HBM)] * 5,
        out_specs=whole,
        out_shape=jax.ShapeDtypeStruct((tokens, d), BF16),
        scratch_shapes=[pltpu.VMEM((tokens, d), F32)]
        + [pltpu.VMEM((tokens, 128), F32)] * 4
        + [pltpu.VMEM((tokens, d), F32)] * 3
        + [pltpu.SemaphoreType.DMA((5,))],
        compiler_params=params(),
        cost_estimate=cost(6 * tokens * cb * steps * d, cb * steps * d * 2, tokens * cb * steps),
        name="lat_second",
    )(toks, toks, book, row, m_col, mean_col, a, b, rows)


def combine_kernel(all_ref, tgt_ref, first_ref, row_ref, loss_ref):
    stats = all_ref[...]
    m, l, w = stats[:, 0, :], stats[:, 1, :], stats[:, 2, :]
    tokens = m.shape[1]
    top = jnp.max(m, axis=0, keepdims=True)
    scale = jnp.exp(m - top)
    total = jnp.sum(l * scale, axis=0, keepdims=True)
    mean = jnp.sum(w * scale, axis=0, keepdims=True) / total
    lse = top + jnp.log(total)
    pack = jnp.concatenate([lse, mean, tgt_ref[...].astype(F32), mean], axis=0)
    row_ref[...] = jnp.broadcast_to(pack[None], row_ref.shape)
    loss = jnp.broadcast_to(lse - jnp.sum(stats[:, 3, :], axis=0, keepdims=True), (8, tokens))
    loss_ref[...] = pltpu.roll(loss, first_ref[0], 1)[:1, : loss_ref.shape[1]]


def combine(stats, tgt, first, groups, count):
    tokens = stats.shape[-1]
    vmem = pl.BlockSpec(memory_space=pltpu.VMEM)
    return pl.pallas_call(
        combine_kernel,
        in_specs=[vmem, vmem, pl.BlockSpec(memory_space=pltpu.SMEM)],
        out_shape=[
            jax.ShapeDtypeStruct((groups, 4, tokens), F32),
            jax.ShapeDtypeStruct((1, count), F32),
        ],
        compiler_params=params(),
        cost_estimate=cost(tokens * 1000, tokens * 800),
        name="combine",
    )(stats, tgt, first)


def book_kernel(sub, batch, s_ref, rows_ref, book_ref, *rest):
    groups = len(rest) - 3
    toks, (out_ref, buf, sem) = rest[:groups], rest[groups:]
    for g in range(groups):
        pltpu.make_async_copy(toks[g], buf.at[g], sem.at[g]).start()
    chunk, d = book_ref.shape
    tokens = buf.shape[1]
    ids = lax.broadcasted_iota(jnp.int32, (sub, tokens), 0) + s_ref[groups]
    out_ref[...] = jnp.zeros_like(out_ref)

    def block(j):
        return book_ref[j * sub : (j + 1) * sub, :]

    def step(i, carry):
        work = [(i * batch + k, j) for k in range(batch) for j in range(chunk // sub)]

        def logits(g, j):
            if j == 0:
                pltpu.make_async_copy(toks[0], buf.at[g], sem.at[g]).wait()
            return dot(block(j), buf[g, :, :d], NT)

        ahead = logits(*work[0])
        for n, (g, j) in enumerate(work):
            logit = ahead
            if n + 1 < len(work):
                ahead = logits(*work[n + 1])
            row = rows_ref[s_ref[g]]
            back = dot(block(j), buf[g, :, d:], NT)
            prob = jnp.exp(logit - row[0:1])
            hit = jnp.where(ids + j * sub == row[2:3].astype(jnp.int32), 1.0, 0.0)
            delta = prob * (back - row[1:2]) + ce_weight * (prob - hit)
            at = slice(j * sub, (j + 1) * sub)
            out_ref[at, :] += dot(delta.astype(BF16), buf[g, :, :d], NN) + dot(
                hit.astype(BF16), buf[g, :, d:], NN
            )
        return carry

    lax.fori_loop(0, groups // batch, step, 0)


def book_grad(scalars, rows, book, toks, sub=1024, batch=1):
    groups = len(toks)
    (tokens, width), (chunk, d) = toks[0].shape, book.shape
    whole = pl.BlockSpec((chunk, d), lambda i, s: (0, 0))
    grid_spec = pltpu.PrefetchScalarGridSpec(
        num_scalar_prefetch=1,
        grid=(1,),
        in_specs=[pl.BlockSpec(rows.shape, lambda i, s: (0, 0, 0)), whole]
        + [pl.BlockSpec(memory_space=pl.ANY)] * groups,
        out_specs=whole,
        scratch_shapes=[
            pltpu.VMEM((groups, tokens, width), BF16),
            pltpu.SemaphoreType.DMA((groups,)),
        ],
    )
    return pl.pallas_call(
        functools.partial(book_kernel, sub, batch),
        grid_spec=grid_spec,
        out_shape=jax.ShapeDtypeStruct((chunk, d), F32),
        compiler_params=params(),
        cost_estimate=cost(
            8 * groups * tokens * chunk * d, groups * tokens * width * 2, groups * tokens * chunk
        ),
        name="book_grad",
    )(scalars, rows, book, *toks)


def spread_kernel(lat_ref, grad_ref, out_ref):
    both = jnp.concatenate([lat_ref[...], grad_ref[...]], axis=1)
    out_ref[...] = jnp.broadcast_to(both[None], out_ref.shape)


def spread(lat, grad, peers):
    count, d = lat.shape
    return pl.pallas_call(
        spread_kernel,
        out_shape=jax.ShapeDtypeStruct((peers, count, 2 * d), BF16),
        compiler_params=params(),
        name="spread",
    )(lat, grad)


def gather_kernel(in_ref, out_ref):
    out_ref[...] = jnp.sum(in_ref[...].astype(F32), axis=0).astype(out_ref.dtype)


def sum_parts(parts):
    return pl.pallas_call(
        gather_kernel,
        out_shape=jax.ShapeDtypeStruct(parts.shape[1:], BF16),
        compiler_params=params(),
        name="sum_parts",
    )(parts)


def in_hbm(*arrays):
    return [pltpu.with_memory_space_constraint(x, pltpu.HBM) for x in arrays]


def per_device(latents, out_grad, targets, codebook):
    peers = lax.axis_size("z") * lax.axis_size("y")
    nx = lax.axis_size("x")
    own_count, d = latents.shape
    code_dev = codebook.shape[0]
    tokens = own_count * peers
    code_pos = lax.axis_index(ZY)
    x_pos, core = lax.axis_index("x"), lax.axis_index("core")
    dp_pos, chunk = x_pos * 2 + core, code_dev // (2 * nx)
    swap = [(0, 1), (1, 0)]
    book = pltpu.with_memory_space_constraint(codebook, pltpu.HBM)

    toks = lax.all_to_all(spread(*in_hbm(latents, out_grad), peers), ZY, 0, 0)
    toks = toks.reshape(tokens, 2 * d)
    local_ids = targets - code_pos * code_dev
    rows = pick_rows(jnp.broadcast_to(local_ids[:, None], (tokens, 128)), book)
    (rows,) = in_hbm(rows)
    places = [lax.rem(x_pos + nx - k, nx) * 2 for k in range(nx)]
    scalars = [p + core for p in places] + [p + 1 - core for p in places]
    scalars += [code_pos * code_dev + dp_pos * chunk]
    scalars = jnp.stack(scalars).astype(jnp.int32)
    own_book = lax.dynamic_slice(codebook, (dp_pos * chunk, 0), (chunk, d))
    packed, m_col, mean_col = local_stats(toks, rows, book, peers)
    m_col, mean_col = in_hbm(m_col, mean_col)
    stats = lax.all_to_all(packed, ZY, 0, 0)
    same = [toks]
    for k in range(1, nx):
        same.append(lax.ppermute(toks, "x", [(i, (i + k) % nx) for i in range(nx)]))
    a, b = lat_first(toks, m_col, mean_col, book)
    shift = lax.rem(tokens - code_pos * own_count, tokens).astype(jnp.int32).reshape(1)
    row, loss = combine(stats, targets[None], shift, 2 * nx, own_count)
    everyone = lax.all_to_all(row, XC, 0, 0)
    part = lat_second(toks, m_col, mean_col, book, *in_hbm(a, b), rows, row)
    part, everyone = lax.optimization_barrier((part, everyone))
    moved = lax.all_to_all(part.reshape(peers, own_count, d), ZY, 0, 0)
    latent_grad = sum_parts(moved)
    token_loss = loss.reshape(own_count)

    other = []
    for piece in same:
        other.append(lax.ppermute(piece, "core", swap))
    codebook_grad = book_grad(scalars, everyone, own_book, same + other)
    return latent_grad, codebook_grad, token_loss


def solution(mesh):
    shape = (mesh.shape["dp"] // 2, 2, mesh.shape["code"] // 4, 4)
    fine = Mesh(mesh.devices.reshape(shape), ("x", "core", "z", "y"))
    dp, code = ("x", "core"), ("z", "y")
    in_specs = (P(dp + code, None), P(dp + code, None), P(dp), P(code, None))
    out_specs = (P(dp + code, None), P(code + dp, None), P(dp + code))
    return jax.shard_map(
        per_device, mesh=fine, in_specs=in_specs, out_specs=out_specs, check_vma=False
    )
```

```python
import functools

import jax
import jax.numpy as jnp
from jax import lax
from jax.experimental import pallas as pl
from jax.experimental.pallas import tpu as pltpu
from jax.sharding import Mesh
from jax.sharding import PartitionSpec as P

ce_weight = 1.0
F32 = jnp.float32
BF16 = jnp.bfloat16
NT = (((1,), (1,)), ((), ()))
NN = (((1,), (0,)), ((), ()))
ZY = ("z", "y")
XC = ("x", "core")
VMEM_LIMIT = 32 << 20


def dot(a, b, dims, precision=None):
    return lax.dot_general(a, b, dims, preferred_element_type=F32, precision=precision)


def params(**kw):
    return pltpu.CompilerParams(vmem_limit_bytes=VMEM_LIMIT, **kw)


def cost(flops, bytes_accessed, trans=0):
    return pl.CostEstimate(flops=flops, bytes_accessed=bytes_accessed, transcendentals=trans)


def pick_kernel(cb, tgt_ref, book_ref, out_ref):
    i = pl.program_id(0)

    @pl.when(i == 0)
    def _():
        out_ref[...] = jnp.zeros_like(out_ref)

    tokens = tgt_ref.shape[0]
    ids = lax.broadcasted_iota(jnp.int32, (tokens, cb), 1) + i * cb
    hit = jnp.where(ids == tgt_ref[:, :1], 1.0, 0.0).astype(BF16)
    out_ref[...] += dot(hit, book_ref[...], NN)


def pick_rows(tgt_cols, book):
    tokens, codes, d = tgt_cols.shape[0], *book.shape
    cb = 2048
    return pl.pallas_call(
        functools.partial(pick_kernel, cb),
        grid=(codes // cb,),
        in_specs=[
            pl.BlockSpec((tokens, 128), lambda i: (0, 0)),
            pl.BlockSpec((cb, d), lambda i: (i, 0)),
        ],
        out_specs=pl.BlockSpec((tokens, d), lambda i: (0, 0)),
        out_shape=pltpu.HBM((tokens, d), F32),
        compiler_params=params(),
        cost_estimate=cost(2 * tokens * codes * d, codes * d * 2),
        name="pick",
    )(tgt_cols, book)


def fold(x):
    return sum(x[:, i : i + 128] for i in range(0, x.shape[1], 128))


def as_row(x):
    return jnp.sum(x.T, axis=0, keepdims=True)


def as_cols(row):
    return jnp.broadcast_to(row, (128, row.shape[1])).T


def stats_kernel(
    steps, sub, lat_ref, grad_ref, book_ref, rows_hbm, out_ref, m_col, mean_col, m_s, l_s, w_s, rows_ref, sem
):
    i = pl.program_id(0)
    load = pltpu.make_async_copy(rows_hbm, rows_ref, sem)

    @pl.when(i == 0)
    def _():
        load.start()
        m_s[...] = jnp.full_like(m_s, -jnp.inf)
        l_s[...] = jnp.zeros_like(l_s)
        w_s[...] = jnp.zeros_like(w_s)

    cb, tokens = book_ref.shape[0], lat_ref.shape[0]
    count = cb // sub

    def scores(ref, j):
        return dot(book_ref[j * sub : (j + 1) * sub, :], ref[...], NT).reshape(sub // 8, 8, tokens)

    m, l, w = m_s[...], l_s[...], w_s[...]
    ahead = scores(lat_ref, 0)
    for j in range(count):
        logit = ahead
        if j + 1 < count:
            ahead = scores(lat_ref, j + 1)
        back = scores(grad_ref, j)
        new = jnp.maximum(m, jnp.max(logit, axis=0))
        factor = jnp.exp(m - new)
        expo = jnp.exp(logit - new[None])
        l = l * factor + jnp.sum(expo, axis=0)
        w = w * factor + jnp.sum(expo * back, axis=0)
        m = new
    m_s[...], l_s[...], w_s[...] = m, l, w

    @pl.when(i == steps - 1)
    def _():
        m = m_s[...]
        top = jnp.max(m, axis=0, keepdims=True)
        scale = jnp.exp(m - top)
        total = jnp.sum(l_s[...] * scale, axis=0, keepdims=True)
        weighted = jnp.sum(w_s[...] * scale, axis=0, keepdims=True)
        load.wait()
        picked = as_row(fold(lat_ref[...].astype(F32) * rows_ref[...]))
        pack = jnp.concatenate([top, total, weighted, picked], axis=0)
        out_ref[...] = jnp.broadcast_to(pack[None], out_ref.shape)
        m_col[...] = as_cols(top)
        mean_col[...] = as_cols(weighted / total)


def local_stats(toks, rows, book, peers, cb=2048, sub=512):
    tokens, (codes, d) = toks.shape[0], book.shape
    steps = codes // cb
    cols = pl.BlockSpec((tokens, 128), lambda i: (0, 0))
    return pl.pallas_call(
        functools.partial(stats_kernel, steps, sub),
        grid=(steps,),
        in_specs=[
            pl.BlockSpec((tokens, d), lambda i: (0, 0)),
            pl.BlockSpec((tokens, d), lambda i: (0, 1)),
            pl.BlockSpec((cb, d), lambda i: (i, 0)),
            pl.BlockSpec(memory_space=pltpu.HBM),
        ],
        out_specs=[pl.BlockSpec((peers, 4, tokens), lambda i: (0, 0, 0)), cols, cols],
        out_shape=[
            jax.ShapeDtypeStruct((peers, 4, tokens), F32),
            pltpu.HBM((tokens, 128), F32),
            pltpu.HBM((tokens, 128), F32),
        ],
        scratch_shapes=[pltpu.VMEM((8, tokens), F32)] * 3
        + [pltpu.VMEM((tokens, d), F32), pltpu.SemaphoreType.DMA],
        compiler_params=params(),
        cost_estimate=cost(4 * tokens * codes * d, codes * d * 2, tokens * codes),
        name="stats",
    )(toks, toks, book, rows)


def lat_step(sub, lat_ref, grad_ref, m_ref, book_ref, outs, weigh):
    count = book_ref.shape[0] // sub

    def block(j):
        return book_ref[j * sub : (j + 1) * sub, :]

    sums = [ref[...] for ref in outs]
    ahead = dot(lat_ref[...], block(0), NT)
    for j in range(count):
        logit = ahead
        if j + 1 < count:
            ahead = dot(lat_ref[...], block(j + 1), NT)
        back = dot(grad_ref[...], block(j), NT)
        terms = weigh(jnp.exp(logit - m_ref[:, :1]), back)
        sums = [x + dot(term.astype(BF16), block(j), NN) for x, term in zip(sums, terms)]
    for ref, x in zip(outs, sums):
        ref[...] = x


def first_kernel(sub, lat_ref, grad_ref, m_ref, mean_ref, book_ref, a_ref, b_ref):
    @pl.when(pl.program_id(0) == 0)
    def _():
        a_ref[...] = jnp.zeros_like(a_ref)
        b_ref[...] = jnp.zeros_like(b_ref)

    def weigh(expo, back):
        return expo * (back - mean_ref[:, :1]), expo

    lat_step(sub, lat_ref, grad_ref, m_ref, book_ref, (a_ref, b_ref), weigh)


def second_kernel(
    steps, sub, lat_ref, grad_ref, book_ref, all_ref, m_hbm, mean_hbm, a_hbm, b_hbm, rows_hbm,
    part_ref, sum_ref, lse_col, mean_col, m_ref, own_mean, a_ref, b_ref, rows_ref, sem,
):
    i = pl.program_id(0)
    pairs = ((m_hbm, m_ref), (mean_hbm, own_mean), (a_hbm, a_ref), (b_hbm, b_ref), (rows_hbm, rows_ref))
    loads = [pltpu.make_async_copy(src, dst, sem.at[n]) for n, (src, dst) in enumerate(pairs)]

    @pl.when(i == 0)
    def _():
        for load in loads:
            load.start()
        lse_col[...] = as_cols(all_ref[0, 0:1, :])
        mean_col[...] = as_cols(all_ref[0, 1:2, :])
        sum_ref[...] = jnp.zeros_like(sum_ref)

    def weigh(prob, back):
        return (prob * (back - mean_col[:, :1]) + ce_weight * prob,)

    lat_step(sub, lat_ref, grad_ref, lse_col, book_ref, (sum_ref,), weigh)

    @pl.when(i == steps - 1)
    def _():
        for load in loads:
            load.wait()
        own = jnp.exp(m_ref[...] - lse_col[...])
        ratio = own * (ce_weight + own_mean[...] - mean_col[...])
        part = own[:, :1] * a_ref[...] + ratio[:, :1] * b_ref[...] - ce_weight * rows_ref[...]
        part_ref[...] = (sum_ref[...] + part).astype(part_ref.dtype)


def lat_specs(tokens, d, cb, first):
    return [
        pl.BlockSpec((tokens, d), lambda i: (0, 0)),
        pl.BlockSpec((tokens, d), lambda i: (0, 1)),
        pl.BlockSpec((tokens, 128), lambda i: (0, 0)),
        pl.BlockSpec((tokens, 128), lambda i: (0, 0)),
        pl.BlockSpec((cb, d), lambda i: (i + first, 0)),
    ]


def lat_first(toks, m_col, mean_col, book, sub=512):
    tokens, (codes, d) = toks.shape[0], book.shape
    steps, cb = 2, codes * 5 // 16
    whole = pl.BlockSpec((tokens, d), lambda i: (0, 0))
    return pl.pallas_call(
        functools.partial(first_kernel, sub),
        grid=(steps,),
        in_specs=lat_specs(tokens, d, cb, 0),
        out_specs=[whole] * 2,
        out_shape=[pltpu.HBM((tokens, d), F32)] * 2,
        compiler_params=params(),
        cost_estimate=cost(8 * tokens * cb * steps * d, cb * steps * d * 2, tokens * cb * steps),
        name="lat_first",
    )(toks, toks, m_col, mean_col, book)


def lat_second(toks, m_col, mean_col, book, a, b, rows, row, sub=512):
    tokens, (codes, d) = toks.shape[0], book.shape
    first, steps, cb = 5, 3, codes // 8
    whole = pl.BlockSpec((tokens, d), lambda i: (0, 0))
    return pl.pallas_call(
        functools.partial(second_kernel, steps, sub),
        grid=(steps,),
        in_specs=[
            pl.BlockSpec((tokens, d), lambda i: (0, 0)),
            pl.BlockSpec((tokens, d), lambda i: (0, 1)),
            pl.BlockSpec((cb, d), lambda i: (i + first, 0)),
            pl.BlockSpec((1, 4, tokens), lambda i: (0, 0, 0)),
        ]
        + [pl.BlockSpec(memory_space=pltpu.HBM)] * 5,
        out_specs=whole,
        out_shape=jax.ShapeDtypeStruct((tokens, d), F32),
        scratch_shapes=[pltpu.VMEM((tokens, d), F32)]
        + [pltpu.VMEM((tokens, 128), F32)] * 4
        + [pltpu.VMEM((tokens, d), F32)] * 3
        + [pltpu.SemaphoreType.DMA((5,))],
        compiler_params=params(),
        cost_estimate=cost(6 * tokens * cb * steps * d, cb * steps * d * 2, tokens * cb * steps),
        name="lat_second",
    )(toks, toks, book, row, m_col, mean_col, a, b, rows)


def combine_kernel(all_ref, tgt_ref, first_ref, row_ref, loss_ref):
    stats = all_ref[...]
    m, l, w = stats[:, 0, :], stats[:, 1, :], stats[:, 2, :]
    tokens = m.shape[1]
    top = jnp.max(m, axis=0, keepdims=True)
    scale = jnp.exp(m - top)
    total = jnp.sum(l * scale, axis=0, keepdims=True)
    mean = jnp.sum(w * scale, axis=0, keepdims=True) / total
    lse = top + jnp.log(total)
    pack = jnp.concatenate([lse, mean, tgt_ref[...].astype(F32), mean], axis=0)
    row_ref[...] = jnp.broadcast_to(pack[None], row_ref.shape)
    loss = jnp.broadcast_to(lse - jnp.sum(stats[:, 3, :], axis=0, keepdims=True), (8, tokens))
    loss_ref[...] = pltpu.roll(loss, first_ref[0], 1)[:1, : loss_ref.shape[1]]


def combine(stats, tgt, first, groups, count):
    tokens = stats.shape[-1]
    vmem = pl.BlockSpec(memory_space=pltpu.VMEM)
    return pl.pallas_call(
        combine_kernel,
        in_specs=[vmem, vmem, pl.BlockSpec(memory_space=pltpu.SMEM)],
        out_shape=[
            jax.ShapeDtypeStruct((groups, 4, tokens), F32),
            jax.ShapeDtypeStruct((1, count), F32),
        ],
        compiler_params=params(),
        cost_estimate=cost(tokens * 1000, tokens * 800),
        name="combine",
    )(stats, tgt, first)


def book_kernel(sub, batch, s_ref, rows_ref, book_ref, *rest):
    groups = len(rest) - 3
    toks, (out_ref, buf, sem) = rest[:groups], rest[groups:]
    for g in range(groups):
        pltpu.make_async_copy(toks[g], buf.at[g], sem.at[g]).start()
    chunk, d = book_ref.shape
    tokens = buf.shape[1]
    ids = lax.broadcasted_iota(jnp.int32, (sub, tokens), 0) + s_ref[groups]
    out_ref[...] = jnp.zeros_like(out_ref)

    def block(j):
        return book_ref[j * sub : (j + 1) * sub, :]

    def step(i, carry):
        work = [(i * batch + k, j) for k in range(batch) for j in range(chunk // sub)]

        def logits(g, j):
            if j == 0:
                pltpu.make_async_copy(toks[0], buf.at[g], sem.at[g]).wait()
            return dot(block(j), buf[g, :, :d], NT)

        ahead = logits(*work[0])
        for n, (g, j) in enumerate(work):
            logit = ahead
            if n + 1 < len(work):
                ahead = logits(*work[n + 1])
            row = rows_ref[s_ref[g]]
            back = dot(block(j), buf[g, :, d:], NT)
            prob = jnp.exp(logit - row[0:1])
            hit = jnp.where(ids + j * sub == row[2:3].astype(jnp.int32), 1.0, 0.0)
            delta = prob * (back - row[1:2]) + ce_weight * (prob - hit)
            at = slice(j * sub, (j + 1) * sub)
            out_ref[at, :] += dot(delta.astype(BF16), buf[g, :, :d], NN) + dot(
                hit.astype(BF16), buf[g, :, d:], NN
            )
        return carry

    lax.fori_loop(0, groups // batch, step, 0)


def book_grad(scalars, rows, book, toks, sub=1024, batch=1):
    groups = len(toks)
    (tokens, width), (chunk, d) = toks[0].shape, book.shape
    whole = pl.BlockSpec((chunk, d), lambda i, s: (0, 0))
    grid_spec = pltpu.PrefetchScalarGridSpec(
        num_scalar_prefetch=1,
        grid=(1,),
        in_specs=[pl.BlockSpec(rows.shape, lambda i, s: (0, 0, 0)), whole]
        + [pl.BlockSpec(memory_space=pl.ANY)] * groups,
        out_specs=whole,
        scratch_shapes=[
            pltpu.VMEM((groups, tokens, width), BF16),
            pltpu.SemaphoreType.DMA((groups,)),
        ],
    )
    return pl.pallas_call(
        functools.partial(book_kernel, sub, batch),
        grid_spec=grid_spec,
        out_shape=jax.ShapeDtypeStruct((chunk, d), F32),
        compiler_params=params(),
        cost_estimate=cost(
            8 * groups * tokens * chunk * d, groups * tokens * width * 2, groups * tokens * chunk
        ),
        name="book_grad",
    )(scalars, rows, book, *toks)


def spread_kernel(lat_ref, grad_ref, out_ref):
    both = jnp.concatenate([lat_ref[...], grad_ref[...]], axis=1)
    out_ref[...] = jnp.broadcast_to(both[None], out_ref.shape)


def spread(lat, grad, peers):
    count, d = lat.shape
    return pl.pallas_call(
        spread_kernel,
        out_shape=jax.ShapeDtypeStruct((peers, count, 2 * d), BF16),
        compiler_params=params(),
        name="spread",
    )(lat, grad)


def gather_kernel(in_ref, out_ref):
    out_ref[...] = jnp.sum(in_ref[...].astype(F32), axis=0).astype(out_ref.dtype)


def sum_parts(parts):
    return pl.pallas_call(
        gather_kernel,
        out_shape=jax.ShapeDtypeStruct(parts.shape[1:], BF16),
        compiler_params=params(),
        name="sum_parts",
    )(parts)


def in_hbm(*arrays):
    return [pltpu.with_memory_space_constraint(x, pltpu.HBM) for x in arrays]


def per_device(latents, out_grad, targets, codebook):
    peers = lax.axis_size("z") * lax.axis_size("y")
    nx = lax.axis_size("x")
    own_count, d = latents.shape
    code_dev = codebook.shape[0]
    tokens = own_count * peers
    code_pos = lax.axis_index(ZY)
    x_pos, core = lax.axis_index("x"), lax.axis_index("core")
    dp_pos, chunk = x_pos * 2 + core, code_dev // (2 * nx)
    swap = [(0, 1), (1, 0)]
    book = pltpu.with_memory_space_constraint(codebook, pltpu.HBM)

    toks = lax.all_to_all(spread(*in_hbm(latents, out_grad), peers), ZY, 0, 0)
    toks = toks.reshape(tokens, 2 * d)
    local_ids = targets - code_pos * code_dev
    rows = pick_rows(jnp.broadcast_to(local_ids[:, None], (tokens, 128)), book)
    (rows,) = in_hbm(rows)
    places = [lax.rem(x_pos + nx - k, nx) * 2 for k in range(nx)]
    scalars = [p + core for p in places] + [p + 1 - core for p in places]
    scalars += [code_pos * code_dev + dp_pos * chunk]
    scalars = jnp.stack(scalars).astype(jnp.int32)
    own_book = lax.dynamic_slice(codebook, (dp_pos * chunk, 0), (chunk, d))
    packed, m_col, mean_col = local_stats(toks, rows, book, peers)
    m_col, mean_col = in_hbm(m_col, mean_col)
    stats = lax.all_to_all(packed, ZY, 0, 0)
    same = [toks]
    for k in range(1, nx):
        same.append(lax.ppermute(toks, "x", [(i, (i + k) % nx) for i in range(nx)]))
    a, b = lat_first(toks, m_col, mean_col, book)
    shift = lax.rem(tokens - code_pos * own_count, tokens).astype(jnp.int32).reshape(1)
    row, loss = combine(stats, targets[None], shift, 2 * nx, own_count)
    everyone = lax.all_to_all(row, XC, 0, 0)
    part = lat_second(toks, m_col, mean_col, book, *in_hbm(a, b), rows, row)
    part, everyone = lax.optimization_barrier((part, everyone))
    moved = lax.all_to_all(part.reshape(peers, own_count, d), ZY, 0, 0)
    latent_grad = sum_parts(moved)
    token_loss = loss.reshape(own_count)

    other = []
    for piece in same:
        other.append(lax.ppermute(piece, "core", swap))
    codebook_grad = book_grad(scalars, everyone, own_book, same + other)
    return latent_grad, codebook_grad, token_loss


def solution(mesh):
    shape = (mesh.shape["dp"] // 2, 2, mesh.shape["code"] // 4, 4)
    fine = Mesh(mesh.devices.reshape(shape), ("x", "core", "z", "y"))
    dp, code = ("x", "core"), ("z", "y")
    in_specs = (P(dp + code, None), P(dp + code, None), P(dp), P(code, None))
    out_specs = (P(dp + code, None), P(code + dp, None), P(dp + code))
    return jax.shard_map(
        per_device, mesh=fine, in_specs=in_specs, out_specs=out_specs, check_vma=False
    )
```

```python
import functools

import jax
import jax.numpy as jnp
from jax import lax
from jax.experimental import pallas as pl
from jax.experimental.pallas import tpu as pltpu
from jax.sharding import Mesh
from jax.sharding import PartitionSpec as P

ce_weight = 1.0
F32 = jnp.float32
BF16 = jnp.bfloat16
NT = (((1,), (1,)), ((), ()))
NN = (((1,), (0,)), ((), ()))
ZY = ("z", "y")
XC = ("x", "core")
VMEM_LIMIT = 32 << 20


def dot(a, b, dims, precision=None):
    return lax.dot_general(a, b, dims, preferred_element_type=F32, precision=precision)


def params(**kw):
    return pltpu.CompilerParams(vmem_limit_bytes=VMEM_LIMIT, **kw)


def cost(flops, bytes_accessed, trans=0):
    return pl.CostEstimate(flops=flops, bytes_accessed=bytes_accessed, transcendentals=trans)


def pick_kernel(cb, tgt_ref, book_ref, out_ref):
    i = pl.program_id(0)

    @pl.when(i == 0)
    def _():
        out_ref[...] = jnp.zeros_like(out_ref)

    tokens = tgt_ref.shape[0]
    ids = lax.broadcasted_iota(jnp.int32, (tokens, cb), 1) + i * cb
    hit = jnp.where(ids == tgt_ref[:, :1], 1.0, 0.0).astype(BF16)
    out_ref[...] += dot(hit, book_ref[...], NN)


def pick_rows(tgt_cols, book):
    tokens, codes, d = tgt_cols.shape[0], *book.shape
    cb = 2048
    return pl.pallas_call(
        functools.partial(pick_kernel, cb),
        grid=(codes // cb,),
        in_specs=[
            pl.BlockSpec((tokens, 128), lambda i: (0, 0)),
            pl.BlockSpec((cb, d), lambda i: (i, 0)),
        ],
        out_specs=pl.BlockSpec((tokens, d), lambda i: (0, 0)),
        out_shape=pltpu.HBM((tokens, d), F32),
        compiler_params=params(),
        cost_estimate=cost(2 * tokens * codes * d, codes * d * 2),
        name="pick",
    )(tgt_cols, book)


def fold(x):
    return sum(x[:, i : i + 128] for i in range(0, x.shape[1], 128))


def as_row(x):
    return jnp.sum(x.T, axis=0, keepdims=True)


def as_cols(row):
    return jnp.broadcast_to(row, (128, row.shape[1])).T


def stats_kernel(
    steps, sub, lat_ref, grad_ref, book_ref, rows_hbm, out_ref, m_s, l_s, w_s, rows_ref, sem
):
    i = pl.program_id(0)
    load = pltpu.make_async_copy(rows_hbm, rows_ref, sem)

    @pl.when(i == 0)
    def _():
        load.start()
        m_s[...] = jnp.full_like(m_s, -jnp.inf)
        l_s[...] = jnp.zeros_like(l_s)
        w_s[...] = jnp.zeros_like(w_s)

    cb, tokens = book_ref.shape[0], lat_ref.shape[0]
    count = cb // sub

    def scores(ref, j):
        return dot(book_ref[j * sub : (j + 1) * sub, :], ref[...], NT).reshape(sub // 8, 8, tokens)

    m, l, w = m_s[...], l_s[...], w_s[...]
    ahead = scores(lat_ref, 0)
    for j in range(count):
        logit = ahead
        if j + 1 < count:
            ahead = scores(lat_ref, j + 1)
        back = scores(grad_ref, j)
        new = jnp.maximum(m, jnp.max(logit, axis=0))
        factor = jnp.exp(m - new)
        expo = jnp.exp(logit - new[None])
        l = l * factor + jnp.sum(expo, axis=0)
        w = w * factor + jnp.sum(expo * back, axis=0)
        m = new
    m_s[...], l_s[...], w_s[...] = m, l, w

    @pl.when(i == steps - 1)
    def _():
        m = m_s[...]
        top = jnp.max(m, axis=0, keepdims=True)
        scale = jnp.exp(m - top)
        total = jnp.sum(l_s[...] * scale, axis=0, keepdims=True)
        weighted = jnp.sum(w_s[...] * scale, axis=0, keepdims=True)
        load.wait()
        picked = as_row(fold(lat_ref[...].astype(F32) * rows_ref[...]))
        pack = jnp.concatenate([top, total, weighted, picked], axis=0)
        out_ref[...] = jnp.broadcast_to(pack[None], out_ref.shape)


def local_stats(toks, rows, book, peers, cb=4096, sub=512):
    tokens, (codes, d) = toks.shape[0], book.shape
    steps = codes // cb
    return pl.pallas_call(
        functools.partial(stats_kernel, steps, sub),
        grid=(steps,),
        in_specs=[
            pl.BlockSpec((tokens, d), lambda i: (0, 0)),
            pl.BlockSpec((tokens, d), lambda i: (0, 1)),
            pl.BlockSpec((cb, d), lambda i: (i, 0)),
            pl.BlockSpec(memory_space=pltpu.HBM),
        ],
        out_specs=pl.BlockSpec((peers, 4, tokens), lambda i: (0, 0, 0)),
        out_shape=jax.ShapeDtypeStruct((peers, 4, tokens), F32),
        scratch_shapes=[pltpu.VMEM((8, tokens), F32)] * 3
        + [pltpu.VMEM((tokens, d), F32), pltpu.SemaphoreType.DMA],
        compiler_params=params(),
        cost_estimate=cost(4 * tokens * codes * d, codes * d * 2, tokens * codes),
        name="stats",
    )(toks, toks, book, rows)


def lat_step(sub, lat_ref, grad_ref, m_ref, book_ref, outs, weigh):
    count = book_ref.shape[0] // sub

    def block(j):
        return book_ref[j * sub : (j + 1) * sub, :]

    sums = [ref[...] for ref in outs]
    ahead = dot(lat_ref[...], block(0), NT)
    for j in range(count):
        logit = ahead
        if j + 1 < count:
            ahead = dot(lat_ref[...], block(j + 1), NT)
        back = dot(grad_ref[...], block(j), NT)
        terms = weigh(jnp.exp(logit - m_ref[:, :1]), back)
        sums = [x + dot(term.astype(BF16), block(j), NN) for x, term in zip(sums, terms)]
    for ref, x in zip(outs, sums):
        ref[...] = x


def first_kernel(sub, lat_ref, grad_ref, book_ref, pack_ref, a_ref, b_ref, m_ref, mean_ref):
    @pl.when(pl.program_id(0) == 0)
    def _():
        m_ref[...] = as_cols(pack_ref[0, 0:1, :])
        mean_ref[...] = as_cols(pack_ref[0, 2:3, :] / pack_ref[0, 1:2, :])
        a_ref[...] = jnp.zeros_like(a_ref)
        b_ref[...] = jnp.zeros_like(b_ref)

    def weigh(expo, back):
        return expo * (back - mean_ref[:, :1]), expo

    lat_step(sub, lat_ref, grad_ref, m_ref, book_ref, (a_ref, b_ref), weigh)


def second_kernel(
    steps, sub, lat_ref, grad_ref, book_ref, pack_ref, all_ref, a_hbm, b_hbm, rows_hbm,
    part_ref, sum_ref, lse_col, mean_col, a_ref, b_ref, rows_ref, sem,
):
    i = pl.program_id(0)
    pairs = ((a_hbm, a_ref), (b_hbm, b_ref), (rows_hbm, rows_ref))
    loads = [pltpu.make_async_copy(src, dst, sem.at[n]) for n, (src, dst) in enumerate(pairs)]

    @pl.when(i == 0)
    def _():
        for load in loads:
            load.start()
        lse_col[...] = as_cols(all_ref[0, 0:1, :])
        mean_col[...] = as_cols(all_ref[0, 1:2, :])
        sum_ref[...] = jnp.zeros_like(sum_ref)

    def weigh(prob, back):
        return (prob * (back - mean_col[:, :1]) + ce_weight * prob,)

    lat_step(sub, lat_ref, grad_ref, lse_col, book_ref, (sum_ref,), weigh)

    @pl.when(i == steps - 1)
    def _():
        for load in loads:
            load.wait()
        own = jnp.exp(pack_ref[0, 0:1, :] - all_ref[0, 0:1, :])
        local = pack_ref[0, 2:3, :] / pack_ref[0, 1:2, :]
        ratio = own * (ce_weight + local - all_ref[0, 1:2, :])
        part = as_cols(own)[:, :1] * a_ref[...] + as_cols(ratio)[:, :1] * b_ref[...]
        part_ref[...] = (sum_ref[...] + part - ce_weight * rows_ref[...]).astype(part_ref.dtype)


def lat_specs(tokens, d, cb, first):
    return [
        pl.BlockSpec((tokens, d), lambda i: (0, 0)),
        pl.BlockSpec((tokens, d), lambda i: (0, 1)),
        pl.BlockSpec((cb, d), lambda i: (i + first, 0)),
        pl.BlockSpec((1, 4, tokens), lambda i: (0, 0, 0)),
    ]


def lat_first(toks, packed, book, part=1, parts=2, cb=2048, sub=512):
    tokens, (codes, d) = toks.shape[0], book.shape
    steps = codes // cb * part // parts
    whole = pl.BlockSpec((tokens, d), lambda i: (0, 0))
    return pl.pallas_call(
        functools.partial(first_kernel, sub),
        grid=(steps,),
        in_specs=lat_specs(tokens, d, cb, 0),
        out_specs=[whole] * 2,
        out_shape=[pltpu.HBM((tokens, d), F32)] * 2,
        scratch_shapes=[pltpu.VMEM((tokens, 128), F32)] * 2,
        compiler_params=params(),
        cost_estimate=cost(8 * tokens * cb * steps * d, cb * steps * d * 2, tokens * cb * steps),
        name="lat_first",
    )(toks, toks, book, packed)


def lat_second(toks, packed, book, a, b, rows, row, part=1, parts=2, cb=4096, sub=512):
    tokens, (codes, d) = toks.shape[0], book.shape
    first = codes // cb * part // parts
    steps = codes // cb - first
    whole = pl.BlockSpec((tokens, d), lambda i: (0, 0))
    return pl.pallas_call(
        functools.partial(second_kernel, steps, sub),
        grid=(steps,),
        in_specs=lat_specs(tokens, d, cb, first)
        + [pl.BlockSpec((1, 4, tokens), lambda i: (0, 0, 0))]
        + [pl.BlockSpec(memory_space=pltpu.HBM)] * 3,
        out_specs=whole,
        out_shape=jax.ShapeDtypeStruct((tokens, d), BF16),
        scratch_shapes=[pltpu.VMEM((tokens, d), F32)]
        + [pltpu.VMEM((tokens, 128), F32)] * 2
        + [pltpu.VMEM((tokens, d), F32)] * 3
        + [pltpu.SemaphoreType.DMA((3,))],
        compiler_params=params(),
        cost_estimate=cost(6 * tokens * cb * steps * d, cb * steps * d * 2, tokens * cb * steps),
        name="lat_second",
    )(toks, toks, book, packed, row, a, b, rows)


def combine_kernel(all_ref, tgt_ref, first_ref, row_ref, loss_ref):
    stats = all_ref[...]
    m, l, w = stats[:, 0, :], stats[:, 1, :], stats[:, 2, :]
    tokens = m.shape[1]
    top = jnp.max(m, axis=0, keepdims=True)
    scale = jnp.exp(m - top)
    total = jnp.sum(l * scale, axis=0, keepdims=True)
    mean = jnp.sum(w * scale, axis=0, keepdims=True) / total
    lse = top + jnp.log(total)
    pack = jnp.concatenate([lse, mean, tgt_ref[...].astype(F32), mean], axis=0)
    row_ref[...] = jnp.broadcast_to(pack[None], row_ref.shape)
    loss = jnp.broadcast_to(lse - jnp.sum(stats[:, 3, :], axis=0, keepdims=True), (8, tokens))
    loss_ref[...] = pltpu.roll(loss, first_ref[0], 1)[:1, : loss_ref.shape[1]]


def combine(stats, tgt, first, groups, count):
    tokens = stats.shape[-1]
    vmem = pl.BlockSpec(memory_space=pltpu.VMEM)
    return pl.pallas_call(
        combine_kernel,
        in_specs=[vmem, vmem, pl.BlockSpec(memory_space=pltpu.SMEM)],
        out_shape=[
            jax.ShapeDtypeStruct((groups, 4, tokens), F32),
            jax.ShapeDtypeStruct((1, count), F32),
        ],
        compiler_params=params(),
        cost_estimate=cost(tokens * 1000, tokens * 800),
        name="combine",
    )(stats, tgt, first)


def book_kernel(sub, batch, s_ref, rows_ref, book_ref, *rest):
    groups = len(rest) - 3
    toks, (out_ref, buf, sem) = rest[:groups], rest[groups:]
    for g in range(groups):
        pltpu.make_async_copy(toks[g], buf.at[g], sem.at[g]).start()
    chunk, d = book_ref.shape
    tokens = buf.shape[1]
    ids = lax.broadcasted_iota(jnp.int32, (sub, tokens), 0) + s_ref[groups]
    out_ref[...] = jnp.zeros_like(out_ref)

    def block(j):
        return book_ref[j * sub : (j + 1) * sub, :]

    def step(i, carry):
        work = [(i * batch + k, j) for k in range(batch) for j in range(chunk // sub)]

        def logits(g, j):
            if j == 0:
                pltpu.make_async_copy(toks[0], buf.at[g], sem.at[g]).wait()
            return dot(block(j), buf[g, :, :d], NT)

        ahead = logits(*work[0])
        for n, (g, j) in enumerate(work):
            logit = ahead
            if n + 1 < len(work):
                ahead = logits(*work[n + 1])
            row = rows_ref[s_ref[g]]
            back = dot(block(j), buf[g, :, d:], NT)
            prob = jnp.exp(logit - row[0:1])
            hit = jnp.where(ids + j * sub == row[2:3].astype(jnp.int32), 1.0, 0.0)
            delta = prob * (back - row[1:2]) + ce_weight * (prob - hit)
            at = slice(j * sub, (j + 1) * sub)
            out_ref[at, :] += dot(delta.astype(BF16), buf[g, :, :d], NN) + dot(
                hit.astype(BF16), buf[g, :, d:], NN
            )
        return carry

    lax.fori_loop(0, groups // batch, step, 0)


def book_grad(scalars, rows, book, toks, sub=1024, batch=1):
    groups = len(toks)
    (tokens, width), (chunk, d) = toks[0].shape, book.shape
    whole = pl.BlockSpec((chunk, d), lambda i, s: (0, 0))
    grid_spec = pltpu.PrefetchScalarGridSpec(
        num_scalar_prefetch=1,
        grid=(1,),
        in_specs=[pl.BlockSpec(rows.shape, lambda i, s: (0, 0, 0)), whole]
        + [pl.BlockSpec(memory_space=pl.ANY)] * groups,
        out_specs=whole,
        scratch_shapes=[
            pltpu.VMEM((groups, tokens, width), BF16),
            pltpu.SemaphoreType.DMA((groups,)),
        ],
    )
    return pl.pallas_call(
        functools.partial(book_kernel, sub, batch),
        grid_spec=grid_spec,
        out_shape=jax.ShapeDtypeStruct((chunk, d), F32),
        compiler_params=params(),
        cost_estimate=cost(
            8 * groups * tokens * chunk * d, groups * tokens * width * 2, groups * tokens * chunk
        ),
        name="book_grad",
    )(scalars, rows, book, *toks)


def spread_kernel(lat_ref, grad_ref, out_ref):
    both = jnp.concatenate([lat_ref[...], grad_ref[...]], axis=1)
    out_ref[...] = jnp.broadcast_to(both[None], out_ref.shape)


def spread(lat, grad, peers):
    count, d = lat.shape
    return pl.pallas_call(
        spread_kernel,
        out_shape=jax.ShapeDtypeStruct((peers, count, 2 * d), BF16),
        compiler_params=params(),
        name="spread",
    )(lat, grad)


def gather_kernel(in_ref, out_ref):
    out_ref[...] = jnp.sum(in_ref[...].astype(F32), axis=0).astype(out_ref.dtype)


def sum_parts(parts):
    return pl.pallas_call(
        gather_kernel,
        out_shape=jax.ShapeDtypeStruct(parts.shape[1:], BF16),
        compiler_params=params(),
        name="sum_parts",
    )(parts)


def in_hbm(*arrays):
    return [pltpu.with_memory_space_constraint(x, pltpu.HBM) for x in arrays]


def per_device(latents, out_grad, targets, codebook):
    peers = lax.axis_size("z") * lax.axis_size("y")
    nx = lax.axis_size("x")
    own_count, d = latents.shape
    code_dev = codebook.shape[0]
    tokens = own_count * peers
    code_pos = lax.axis_index(ZY)
    x_pos, core = lax.axis_index("x"), lax.axis_index("core")
    dp_pos, chunk = x_pos * 2 + core, code_dev // (2 * nx)
    swap = [(0, 1), (1, 0)]
    book = pltpu.with_memory_space_constraint(codebook, pltpu.HBM)

    toks = lax.all_to_all(spread(*in_hbm(latents, out_grad), peers), ZY, 0, 0)
    toks = toks.reshape(tokens, 2 * d)
    local_ids = targets - code_pos * code_dev
    rows = pick_rows(jnp.broadcast_to(local_ids[:, None], (tokens, 128)), book)
    (rows,) = in_hbm(rows)
    places = [lax.rem(x_pos + nx - k, nx) * 2 for k in range(nx)]
    scalars = [p + core for p in places] + [p + 1 - core for p in places]
    scalars += [code_pos * code_dev + dp_pos * chunk]
    scalars = jnp.stack(scalars).astype(jnp.int32)
    own_book = lax.dynamic_slice(codebook, (dp_pos * chunk, 0), (chunk, d))
    packed = local_stats(toks, rows, book, peers)
    stats = lax.all_to_all(packed, ZY, 0, 0)
    same = [toks]
    for k in range(1, nx):
        same.append(lax.ppermute(toks, "x", [(i, (i + k) % nx) for i in range(nx)]))
    a, b = lat_first(toks, packed, book)
    shift = lax.rem(tokens - code_pos * own_count, tokens).astype(jnp.int32).reshape(1)
    row, loss = combine(stats, targets[None], shift, 2 * nx, own_count)
    everyone = lax.all_to_all(row, XC, 0, 0)
    part = lat_second(toks, packed, book, *in_hbm(a, b), rows, row)
    part, everyone = lax.optimization_barrier((part, everyone))
    moved = lax.all_to_all(part.reshape(peers, own_count, d), ZY, 0, 0)
    latent_grad = sum_parts(moved)
    token_loss = loss.reshape(own_count)

    other = []
    for piece in same:
        other.append(lax.ppermute(piece, "core", swap))
    codebook_grad = book_grad(scalars, everyone, own_book, same + other)
    return latent_grad, codebook_grad, token_loss


def solution(mesh):
    shape = (mesh.shape["dp"] // 2, 2, mesh.shape["code"] // 4, 4)
    fine = Mesh(mesh.devices.reshape(shape), ("x", "core", "z", "y"))
    dp, code = ("x", "core"), ("z", "y")
    in_specs = (P(dp + code, None), P(dp + code, None), P(dp), P(code, None))
    out_specs = (P(dp + code, None), P(code + dp, None), P(dp + code))
    return jax.shard_map(
        per_device, mesh=fine, in_specs=in_specs, out_specs=out_specs, check_vma=False
    )
```

```python
import functools

import jax
import jax.numpy as jnp
from jax import lax
from jax.experimental import pallas as pl
from jax.experimental.pallas import tpu as pltpu
from jax.sharding import Mesh
from jax.sharding import PartitionSpec as P

ce_weight = 1.0
F32 = jnp.float32
BF16 = jnp.bfloat16
NT = (((1,), (1,)), ((), ()))
NN = (((1,), (0,)), ((), ()))
ZY = ("z", "y")
XC = ("x", "core")
VMEM_LIMIT = 32 << 20


def dot(a, b, dims, precision=None):
    return lax.dot_general(a, b, dims, preferred_element_type=F32, precision=precision)


def params(**kw):
    return pltpu.CompilerParams(vmem_limit_bytes=VMEM_LIMIT, **kw)


def cost(flops, bytes_accessed, trans=0):
    return pl.CostEstimate(flops=flops, bytes_accessed=bytes_accessed, transcendentals=trans)


def pick_kernel(cb, tgt_ref, book_ref, out_ref):
    i = pl.program_id(0)

    @pl.when(i == 0)
    def _():
        out_ref[...] = jnp.zeros_like(out_ref)

    tokens = tgt_ref.shape[0]
    ids = lax.broadcasted_iota(jnp.int32, (tokens, cb), 1) + i * cb
    hit = jnp.where(ids == tgt_ref[:, :1], 1.0, 0.0).astype(BF16)
    out_ref[...] += dot(hit, book_ref[...], NN)


def pick_rows(tgt_cols, book):
    tokens, codes, d = tgt_cols.shape[0], *book.shape
    cb = 2048
    return pl.pallas_call(
        functools.partial(pick_kernel, cb),
        grid=(codes // cb,),
        in_specs=[
            pl.BlockSpec((tokens, 128), lambda i: (0, 0)),
            pl.BlockSpec((cb, d), lambda i: (i, 0)),
        ],
        out_specs=pl.BlockSpec((tokens, d), lambda i: (0, 0)),
        out_shape=pltpu.HBM((tokens, d), F32),
        compiler_params=params(),
        cost_estimate=cost(2 * tokens * codes * d, codes * d * 2),
        name="pick",
    )(tgt_cols, book)


def fold(x):
    return sum(x[:, i : i + 128] for i in range(0, x.shape[1], 128))


def as_row(x):
    return jnp.sum(x.T, axis=0, keepdims=True)


def as_cols(row):
    return jnp.broadcast_to(row, (128, row.shape[1])).T


def stats_kernel(
    steps, sub, lat_ref, grad_ref, book_ref, rows_hbm, out_ref, m_s, l_s, w_s, rows_ref, sem
):
    i = pl.program_id(0)
    load = pltpu.make_async_copy(rows_hbm, rows_ref, sem)

    @pl.when(i == 0)
    def _():
        load.start()
        m_s[...] = jnp.full_like(m_s, -jnp.inf)
        l_s[...] = jnp.zeros_like(l_s)
        w_s[...] = jnp.zeros_like(w_s)

    cb, tokens = book_ref.shape[0], lat_ref.shape[0]
    count = cb // sub

    def scores(ref, j):
        return dot(book_ref[j * sub : (j + 1) * sub, :], ref[...], NT).reshape(sub // 8, 8, tokens)

    m, l, w = m_s[...], l_s[...], w_s[...]
    ahead = scores(lat_ref, 0)
    for j in range(count):
        logit = ahead
        if j + 1 < count:
            ahead = scores(lat_ref, j + 1)
        back = scores(grad_ref, j)
        new = jnp.maximum(m, jnp.max(logit, axis=0))
        factor = jnp.exp(m - new)
        expo = jnp.exp(logit - new[None])
        l = l * factor + jnp.sum(expo, axis=0)
        w = w * factor + jnp.sum(expo * back, axis=0)
        m = new
    m_s[...], l_s[...], w_s[...] = m, l, w

    @pl.when(i == steps - 1)
    def _():
        m = m_s[...]
        top = jnp.max(m, axis=0, keepdims=True)
        scale = jnp.exp(m - top)
        total = jnp.sum(l_s[...] * scale, axis=0, keepdims=True)
        weighted = jnp.sum(w_s[...] * scale, axis=0, keepdims=True)
        load.wait()
        picked = as_row(fold(lat_ref[...].astype(F32) * rows_ref[...]))
        pack = jnp.concatenate([top, total, weighted, picked], axis=0)
        out_ref[...] = jnp.broadcast_to(pack[None], out_ref.shape)


def local_stats(toks, rows, book, peers, cb=4096, sub=512):
    tokens, (codes, d) = toks.shape[0], book.shape
    steps = codes // cb
    return pl.pallas_call(
        functools.partial(stats_kernel, steps, sub),
        grid=(steps,),
        in_specs=[
            pl.BlockSpec((tokens, d), lambda i: (0, 0)),
            pl.BlockSpec((tokens, d), lambda i: (0, 1)),
            pl.BlockSpec((cb, d), lambda i: (i, 0)),
            pl.BlockSpec(memory_space=pltpu.HBM),
        ],
        out_specs=pl.BlockSpec((peers, 4, tokens), lambda i: (0, 0, 0)),
        out_shape=jax.ShapeDtypeStruct((peers, 4, tokens), F32),
        scratch_shapes=[pltpu.VMEM((8, tokens), F32)] * 3
        + [pltpu.VMEM((tokens, d), F32), pltpu.SemaphoreType.DMA],
        compiler_params=params(),
        cost_estimate=cost(4 * tokens * codes * d, codes * d * 2, tokens * codes),
        name="stats",
    )(toks, toks, book, rows)


def lat_step(sub, lat_ref, grad_ref, m_ref, book_ref, outs, weigh):
    count = book_ref.shape[0] // sub

    def block(j):
        return book_ref[j * sub : (j + 1) * sub, :]

    sums = [ref[...] for ref in outs]
    ahead = dot(lat_ref[...], block(0), NT)
    for j in range(count):
        logit = ahead
        if j + 1 < count:
            ahead = dot(lat_ref[...], block(j + 1), NT)
        back = dot(grad_ref[...], block(j), NT)
        terms = weigh(jnp.exp(logit - m_ref[:, :1]), back)
        sums = [x + dot(term.astype(BF16), block(j), NN) for x, term in zip(sums, terms)]
    for ref, x in zip(outs, sums):
        ref[...] = x


def first_kernel(sub, lat_ref, grad_ref, book_ref, pack_ref, a_ref, b_ref, m_ref, mean_ref):
    @pl.when(pl.program_id(0) == 0)
    def _():
        m_ref[...] = as_cols(pack_ref[0, 0:1, :])
        mean_ref[...] = as_cols(pack_ref[0, 2:3, :] / pack_ref[0, 1:2, :])
        a_ref[...] = jnp.zeros_like(a_ref)
        b_ref[...] = jnp.zeros_like(b_ref)

    def weigh(expo, back):
        return expo * (back - mean_ref[:, :1]), expo

    lat_step(sub, lat_ref, grad_ref, m_ref, book_ref, (a_ref, b_ref), weigh)


def second_kernel(
    first, sub, lat_ref, grad_ref, pack_ref, all_ref, book_hbm, a_hbm, b_hbm, rows_hbm,
    part_ref, sum_ref, lse_col, mean_col, book_ref, a_ref, b_ref, rows_ref, sem,
):
    near = pltpu.make_async_copy(book_hbm.at[pl.ds(first, book_ref.shape[0])], book_ref, sem.at[3])
    near.start()
    pairs = ((a_hbm, a_ref), (b_hbm, b_ref), (rows_hbm, rows_ref))
    loads = [pltpu.make_async_copy(src, dst, sem.at[n]) for n, (src, dst) in enumerate(pairs)]

    for load in loads:
        load.start()
    lse_col[...] = as_cols(all_ref[0, 0:1, :])
    mean_col[...] = as_cols(all_ref[0, 1:2, :])
    sum_ref[...] = jnp.zeros_like(sum_ref)
    near.wait()

    def weigh(prob, back):
        return (prob * (back - mean_col[:, :1]) + ce_weight * prob,)

    lat_step(sub, lat_ref, grad_ref, lse_col, book_ref, (sum_ref,), weigh)
    for load in loads:
        load.wait()
    own = jnp.exp(pack_ref[0, 0:1, :] - all_ref[0, 0:1, :])
    local = pack_ref[0, 2:3, :] / pack_ref[0, 1:2, :]
    ratio = own * (ce_weight + local - all_ref[0, 1:2, :])
    part = as_cols(own)[:, :1] * a_ref[...] + as_cols(ratio)[:, :1] * b_ref[...]
    part_ref[...] = (sum_ref[...] + part - ce_weight * rows_ref[...]).astype(part_ref.dtype)


def lat_specs(tokens, d, cb, first):
    return [
        pl.BlockSpec((tokens, d), lambda i: (0, 0)),
        pl.BlockSpec((tokens, d), lambda i: (0, 1)),
        pl.BlockSpec((cb, d), lambda i: (i + first, 0)),
        pl.BlockSpec((1, 4, tokens), lambda i: (0, 0, 0)),
    ]


def lat_first(toks, packed, book, sub=512):
    tokens, (codes, d) = toks.shape[0], book.shape
    steps, cb = 2, codes * 5 // 16
    whole = pl.BlockSpec((tokens, d), lambda i: (0, 0))
    return pl.pallas_call(
        functools.partial(first_kernel, sub),
        grid=(steps,),
        in_specs=lat_specs(tokens, d, cb, 0),
        out_specs=[whole] * 2,
        out_shape=[pltpu.HBM((tokens, d), F32)] * 2,
        scratch_shapes=[pltpu.VMEM((tokens, 128), F32)] * 2,
        compiler_params=params(),
        cost_estimate=cost(8 * tokens * cb * steps * d, cb * steps * d * 2, tokens * cb * steps),
        name="lat_first",
    )(toks, toks, book, packed)


def lat_second(toks, packed, book, a, b, rows, row, sub=512):
    tokens, (codes, d) = toks.shape[0], book.shape
    first = codes * 5 // 8
    count = codes - first
    whole = pl.BlockSpec((tokens, d), lambda i: (0, 0))
    return pl.pallas_call(
        functools.partial(second_kernel, first, sub),
        grid=(1,),
        in_specs=[
            pl.BlockSpec((tokens, d), lambda i: (0, 0)),
            pl.BlockSpec((tokens, d), lambda i: (0, 1)),
        ]
        + [pl.BlockSpec((1, 4, tokens), lambda i: (0, 0, 0))] * 2
        + [pl.BlockSpec(memory_space=pltpu.HBM)] * 4,
        out_specs=whole,
        out_shape=jax.ShapeDtypeStruct((tokens, d), BF16),
        scratch_shapes=[pltpu.VMEM((tokens, d), F32)]
        + [pltpu.VMEM((tokens, 128), F32)] * 2
        + [pltpu.VMEM((count, d), BF16)]
        + [pltpu.VMEM((tokens, d), F32)] * 3
        + [pltpu.SemaphoreType.DMA((4,))],
        compiler_params=params(),
        cost_estimate=cost(6 * tokens * count * d, count * d * 2, tokens * count),
        name="lat_second",
    )(toks, toks, packed, row, book, a, b, rows)


def combine_kernel(all_ref, tgt_ref, first_ref, row_ref, loss_ref):
    stats = all_ref[...]
    m, l, w = stats[:, 0, :], stats[:, 1, :], stats[:, 2, :]
    tokens = m.shape[1]
    top = jnp.max(m, axis=0, keepdims=True)
    scale = jnp.exp(m - top)
    total = jnp.sum(l * scale, axis=0, keepdims=True)
    mean = jnp.sum(w * scale, axis=0, keepdims=True) / total
    lse = top + jnp.log(total)
    pack = jnp.concatenate([lse, mean, tgt_ref[...].astype(F32), mean], axis=0)
    row_ref[...] = jnp.broadcast_to(pack[None], row_ref.shape)
    loss = jnp.broadcast_to(lse - jnp.sum(stats[:, 3, :], axis=0, keepdims=True), (8, tokens))
    loss_ref[...] = pltpu.roll(loss, first_ref[0], 1)[:1, : loss_ref.shape[1]]


def combine(stats, tgt, first, groups, count):
    tokens = stats.shape[-1]
    vmem = pl.BlockSpec(memory_space=pltpu.VMEM)
    return pl.pallas_call(
        combine_kernel,
        in_specs=[vmem, vmem, pl.BlockSpec(memory_space=pltpu.SMEM)],
        out_shape=[
            jax.ShapeDtypeStruct((groups, 4, tokens), F32),
            jax.ShapeDtypeStruct((1, count), F32),
        ],
        compiler_params=params(),
        cost_estimate=cost(tokens * 1000, tokens * 800),
        name="combine",
    )(stats, tgt, first)


def book_kernel(sub, batch, s_ref, rows_ref, book_ref, *rest):
    groups = len(rest) - 3
    toks, (out_ref, buf, sem) = rest[:groups], rest[groups:]
    for g in range(groups):
        pltpu.make_async_copy(toks[g], buf.at[g], sem.at[g]).start()
    chunk, d = book_ref.shape
    tokens = buf.shape[1]
    ids = lax.broadcasted_iota(jnp.int32, (sub, tokens), 0) + s_ref[groups]
    out_ref[...] = jnp.zeros_like(out_ref)

    def block(j):
        return book_ref[j * sub : (j + 1) * sub, :]

    def step(i, carry):
        work = [(i * batch + k, j) for k in range(batch) for j in range(chunk // sub)]

        def logits(g, j):
            if j == 0:
                pltpu.make_async_copy(toks[0], buf.at[g], sem.at[g]).wait()
            return dot(block(j), buf[g, :, :d], NT)

        ahead = logits(*work[0])
        for n, (g, j) in enumerate(work):
            logit = ahead
            if n + 1 < len(work):
                ahead = logits(*work[n + 1])
            row = rows_ref[s_ref[g]]
            back = dot(block(j), buf[g, :, d:], NT)
            prob = jnp.exp(logit - row[0:1])
            hit = jnp.where(ids + j * sub == row[2:3].astype(jnp.int32), 1.0, 0.0)
            delta = prob * (back - row[1:2]) + ce_weight * (prob - hit)
            at = slice(j * sub, (j + 1) * sub)
            out_ref[at, :] += dot(delta.astype(BF16), buf[g, :, :d], NN) + dot(
                hit.astype(BF16), buf[g, :, d:], NN
            )
        return carry

    lax.fori_loop(0, groups // batch, step, 0)


def book_grad(scalars, rows, book, toks, sub=1024, batch=1):
    groups = len(toks)
    (tokens, width), (chunk, d) = toks[0].shape, book.shape
    whole = pl.BlockSpec((chunk, d), lambda i, s: (0, 0))
    grid_spec = pltpu.PrefetchScalarGridSpec(
        num_scalar_prefetch=1,
        grid=(1,),
        in_specs=[pl.BlockSpec(rows.shape, lambda i, s: (0, 0, 0)), whole]
        + [pl.BlockSpec(memory_space=pl.ANY)] * groups,
        out_specs=whole,
        scratch_shapes=[
            pltpu.VMEM((groups, tokens, width), BF16),
            pltpu.SemaphoreType.DMA((groups,)),
        ],
    )
    return pl.pallas_call(
        functools.partial(book_kernel, sub, batch),
        grid_spec=grid_spec,
        out_shape=jax.ShapeDtypeStruct((chunk, d), F32),
        compiler_params=params(),
        cost_estimate=cost(
            8 * groups * tokens * chunk * d, groups * tokens * width * 2, groups * tokens * chunk
        ),
        name="book_grad",
    )(scalars, rows, book, *toks)


def spread_kernel(lat_ref, grad_ref, out_ref):
    both = jnp.concatenate([lat_ref[...], grad_ref[...]], axis=1)
    out_ref[...] = jnp.broadcast_to(both[None], out_ref.shape)


def spread(lat, grad, peers):
    count, d = lat.shape
    return pl.pallas_call(
        spread_kernel,
        out_shape=jax.ShapeDtypeStruct((peers, count, 2 * d), BF16),
        compiler_params=params(),
        name="spread",
    )(lat, grad)


def gather_kernel(in_ref, out_ref):
    out_ref[...] = jnp.sum(in_ref[...].astype(F32), axis=0).astype(out_ref.dtype)


def sum_parts(parts):
    return pl.pallas_call(
        gather_kernel,
        out_shape=jax.ShapeDtypeStruct(parts.shape[1:], BF16),
        compiler_params=params(),
        name="sum_parts",
    )(parts)


def in_hbm(*arrays):
    return [pltpu.with_memory_space_constraint(x, pltpu.HBM) for x in arrays]


def per_device(latents, out_grad, targets, codebook):
    peers = lax.axis_size("z") * lax.axis_size("y")
    nx = lax.axis_size("x")
    own_count, d = latents.shape
    code_dev = codebook.shape[0]
    tokens = own_count * peers
    code_pos = lax.axis_index(ZY)
    x_pos, core = lax.axis_index("x"), lax.axis_index("core")
    dp_pos, chunk = x_pos * 2 + core, code_dev // (2 * nx)
    swap = [(0, 1), (1, 0)]
    book = pltpu.with_memory_space_constraint(codebook, pltpu.HBM)

    toks = lax.all_to_all(spread(*in_hbm(latents, out_grad), peers), ZY, 0, 0)
    toks = toks.reshape(tokens, 2 * d)
    local_ids = targets - code_pos * code_dev
    rows = pick_rows(jnp.broadcast_to(local_ids[:, None], (tokens, 128)), book)
    (rows,) = in_hbm(rows)
    places = [lax.rem(x_pos + nx - k, nx) * 2 for k in range(nx)]
    scalars = [p + core for p in places] + [p + 1 - core for p in places]
    scalars += [code_pos * code_dev + dp_pos * chunk]
    scalars = jnp.stack(scalars).astype(jnp.int32)
    own_book = lax.dynamic_slice(codebook, (dp_pos * chunk, 0), (chunk, d))
    packed = local_stats(toks, rows, book, peers)
    stats = lax.all_to_all(packed, ZY, 0, 0)
    same = [toks]
    for k in range(1, nx):
        same.append(lax.ppermute(toks, "x", [(i, (i + k) % nx) for i in range(nx)]))
    a, b = lat_first(toks, packed, book)
    shift = lax.rem(tokens - code_pos * own_count, tokens).astype(jnp.int32).reshape(1)
    row, loss = combine(stats, targets[None], shift, 2 * nx, own_count)
    everyone = lax.all_to_all(row, XC, 0, 0)
    part = lat_second(toks, packed, book, *in_hbm(a, b), rows, row)
    part, everyone = lax.optimization_barrier((part, everyone))
    moved = lax.all_to_all(part.reshape(peers, own_count, d), ZY, 0, 0)
    latent_grad = sum_parts(moved)
    token_loss = loss.reshape(own_count)

    other = []
    for piece in same:
        other.append(lax.ppermute(piece, "core", swap))
    codebook_grad = book_grad(scalars, everyone, own_book, same + other)
    return latent_grad, codebook_grad, token_loss


def solution(mesh):
    shape = (mesh.shape["dp"] // 2, 2, mesh.shape["code"] // 4, 4)
    fine = Mesh(mesh.devices.reshape(shape), ("x", "core", "z", "y"))
    dp, code = ("x", "core"), ("z", "y")
    in_specs = (P(dp + code, None), P(dp + code, None), P(dp), P(code, None))
    out_specs = (P(dp + code, None), P(code + dp, None), P(dp + code))
    return jax.shard_map(
        per_device, mesh=fine, in_specs=in_specs, out_specs=out_specs, check_vma=False
    )
```
